32 devices in a mesh: seq: 4 (over x, core), tp: 8 (over z, y).
Axes of the slice: x: 2, y: 2, z: 4, core: 2. Of those that a mesh axis runs over, the one named last changes fastest.
Arguments:
- hidden_in: bfloat16 [2048, 3584], P('seq', 'tp'), may hold values from -6 to 6
- mamba_gain: float32 [3584], replicated, may hold values from 0.1 to 1.9
- w_xz: bfloat16 [2, 1536, 3584], P(None, 'tp'), may hold values from -0.09375 to 0.09375
- w_bc: bfloat16 [3584, 128], replicated, may hold values from -0.09375 to 0.09375
- w_dt: bfloat16 [24, 3584], P('tp'), may hold values from -0.09375 to 0.09375
- dt_bias: float32 [24], P('tp'), may hold values from -2 to 0
- decay_rate: float32 [24], P('tp'), may hold values from 0.00024414062 to 0.3
- conv_x: float32 [4, 1536], P(None, 'tp'), may hold values from -3 to 3
- conv_bc: float32 [4, 128], replicated, may hold values from -3 to 3
- skip_gain: float32 [24], P('tp'), may hold values from 0.5 to 1.5
- inner_gain: float32 [1536], P('tp'), may hold values from 0.1 to 1.9
- w_out: bfloat16 [1536, 3584], P('tp'), may hold values from -0.15625 to 0.15625
- attn_gain: float32 [3584], replicated, may hold values from 0.1 to 1.9
- w_qkv: bfloat16 [3, 1792, 3584], P(None, 'tp'), may hold values from -0.13363062 to 0.13363062
- w_o: bfloat16 [1792, 3584], P('tp'), may hold values from -0.125 to 0.125
- seg_ids: int32 [2048], P('seq'), may hold values from 0 to 3, as said below
- pad_mask: int32 [2048], P('seq'), may hold values from 0 to 1, as said below
- tenant_bounds: int32 [4, 2], replicated, may hold values from 0 to 2048, as said below
Outputs:
- hidden_out: bfloat16 [2048, 3584], P('seq', 'tp')
- kv_cache: bfloat16 [2, 1792, 2048], P(None, 'tp', 'seq')
- tenant_states: float32 [4, 24, 64, 64], P(None, 'tp')
The draws below stay inside these ranges and needn't reach their ends.
Inputs may be any that keep to these rules, and one draw needn't show every extreme that they name: seg_ids never falls along the tokens; each tenant is one run of at least 128 tokens. `pad_mask`: each tenant's padding is its last tokens, at least one and at most a quarter of its run. `tenant_bounds`: row t holds where tenant t's run in seg_ids starts and one past where it ends; the runs follow one another and cover all 2048 tokens.
All inputs are finite; a program needn't handle non-finite values.
Results may differ from the reference program's by a relative error of at most 0.017.
Values may be sent and summed in bfloat16 or wider, within the bound.
No kernel may reach another device: no remote copies, remote signals or barrier semaphores. Data moves between devices by JAX's collectives and lax.ppermute only.
A program may use at most 128 MiB of HBM per device.

```python
import math
import jax
import jax.numpy as jnp
from jax import lax

D = 3584
HEADDIM = 64
STATE = 64
CONV = 4
HEAD_SIZE = 224
TENANTS = 4
MHEADS = 24
INNER = 1536
HEADS = 8
ATT = 1792
TOKENS = 2048


def tenant_layout(key):
    base_len = TOKENS // 16
    spare = TOKENS - TENANTS * base_len
    cut_points = jnp.sort(jax.random.randint(jax.random.fold_in(key, 11), (TENANTS - 1,), 0, spare + 1))
    edges = jnp.concatenate([jnp.zeros((1,), jnp.int32), cut_points.astype(jnp.int32), jnp.full((1,), spare, jnp.int32)])
    lengths = edges[1:] - edges[:-1] + base_len
    run_ends = jnp.cumsum(lengths).astype(jnp.int32)
    run_starts = run_ends - lengths
    pad_counts = jax.random.randint(jax.random.fold_in(key, 12), (TENANTS,), 1, lengths // 4 + 1).astype(jnp.int32)
    places = jnp.arange(TOKENS, dtype=jnp.int32)
    tenant_row = jnp.sum((places[:, None] >= run_starts[None, :]).astype(jnp.int32), axis=1) - 1
    real_end = run_ends - pad_counts
    live_rows = (places < real_end[tenant_row]).astype(jnp.int32)
    return (tenant_row.astype(jnp.int32), live_rows, jnp.stack([run_starts, run_ends], axis=1).astype(jnp.int32))


def draw_seg_ids(key, part):
    return tenant_layout(key)[0]


def draw_pad_mask(key, part):
    return tenant_layout(key)[1]


def draw_tenant_bounds(key, part):
    return tenant_layout(key)[2]


def draw_hidden_in(key, part):
    rows = jax.random.normal(jax.random.fold_in(key, 1), (TOKENS, D), jnp.float32)
    return jnp.clip(rows, -6.0, 6.0).astype(jnp.bfloat16)


def draw_w_qkv(key, part):
    scale = D ** (-0.5)
    entries = jax.random.normal(jax.random.fold_in(key, 3), (3, ATT, D), jnp.float32) * scale
    return jnp.clip(entries, -8.0 * scale, 8.0 * scale).astype(jnp.bfloat16)


def level_of(stream_key, dims, split, smallest, high):
    def one(dim, blocks):
        draws = jax.random.uniform(jax.random.fold_in(jax.random.fold_in(stream_key, 6), dim), (blocks,), jnp.float32, smallest / len(split), high / len(split))
        return jnp.repeat(jnp.exp(draws), dims[dim] // blocks).reshape((-1,) + (1,) * (len(dims) - dim - 1))

    gain = one(*split[0])
    for cut in split[1:]:
        gain = gain * one(*cut)
    return gain


def normal_values(key, shape, width, limit, split=(), held_as=jnp.bfloat16):
    values = width * jax.random.normal(key, shape, jnp.float32)
    if split:
        values = values * level_of(key, shape, split, -0.22, 0.18)
    return jnp.clip(values, -limit, limit).astype(held_as)


def setup_inputs(seed: int = 0) -> dict:
    key_of = jax.random.split(jax.random.key(seed), 19)
    return {
        "hidden_in": draw_hidden_in(jax.random.fold_in(key_of[18], 71), 0),
        "mamba_gain": jnp.clip(1.0 + 0.18 * jax.random.normal(key_of[1], (D,), jnp.float32), 0.1, 1.9),
        "w_xz": normal_values(key_of[2], (2, INNER, D), D ** -0.5, 0.09375, ((1, 8),)),
        "w_bc": normal_values(key_of[3], (D, 2 * STATE), D ** -0.5, 0.09375),
        "w_dt": normal_values(key_of[4], (MHEADS, D), D ** -0.5, 0.09375, ((0, 8),)),
        "dt_bias": jnp.clip(-2.0 + 2.0 * jax.random.uniform(key_of[5], (MHEADS,), jnp.float32) ** level_of(key_of[5], (MHEADS,), ((0, 8),), -0.2, 0.2), -2.0, 0.0),
        "decay_rate": jnp.clip(jnp.exp(math.log(0.3) - 7.1137934 * jax.random.uniform(key_of[6], (MHEADS,), jnp.float32) ** level_of(key_of[6], (MHEADS,), ((0, 8),), -0.2, 0.2)), 0.00024414062, 0.3),
        "conv_x": normal_values(key_of[7], (CONV, INNER), 0.5, 3.0, ((1, 8),), jnp.float32),
        "conv_bc": normal_values(key_of[8], (CONV, 2 * STATE), 0.5, 3.0, (), jnp.float32),
        "skip_gain": jnp.clip(0.5 + 1.0 * jax.random.uniform(key_of[9], (MHEADS,), jnp.float32) ** level_of(key_of[9], (MHEADS,), ((0, 8),), -0.2, 0.2), 0.5, 1.5),
        "inner_gain": jnp.clip(1.0 + 0.18 * jax.random.normal(key_of[10], (INNER,), jnp.float32), 0.1, 1.9),
        "w_out": normal_values(key_of[11], (INNER, D), INNER ** -0.5, 0.15625, ((0, 8),)),
        "attn_gain": jnp.clip(1.0 + 0.18 * jax.random.normal(key_of[12], (D,), jnp.float32), 0.1, 1.9),
        "w_qkv": draw_w_qkv(jax.random.fold_in(key_of[18], 71), 0),
        "w_o": normal_values(key_of[14], (ATT, D), ATT ** -0.5, 0.125, ((0, 8),)),
        "seg_ids": draw_seg_ids(jax.random.fold_in(key_of[18], 71), 0),
        "pad_mask": draw_pad_mask(jax.random.fold_in(key_of[18], 71), 0),
        "tenant_bounds": draw_tenant_bounds(jax.random.fold_in(key_of[18], 71), 0),
    }


def rms_scale(rows):
    return lax.rsqrt(lax.optimization_barrier(jnp.mean(rows * rows, axis=-1, keepdims=True)) + 1e-05)

def times_rows(left, weights):
    return lax.dot_general(left, weights, (((1,), (1,)), ((), ())), preferred_element_type=jnp.float32)

def reference(hidden_in, mamba_gain, w_xz, w_bc, w_dt, dt_bias, decay_rate, conv_x, conv_bc, skip_gain, inner_gain, w_out, attn_gain, w_qkv, w_o, seg_ids, pad_mask, tenant_bounds):
    wide = hidden_in.astype(jnp.float32)
    normed = (wide * rms_scale(wide) * mamba_gain).astype(jnp.bfloat16)
    projected = times_rows(normed, w_xz.reshape(2 * INNER, D))
    bc_raw = jnp.dot(normed, w_bc, preferred_element_type=jnp.float32)
    live_rows = pad_mask.astype(jnp.float32)
    step_size = jax.nn.softplus(times_rows(normed, w_dt) + dt_bias) * live_rows[:, None]
    raw_input = jnp.concatenate([projected[:, :INNER], bc_raw], axis=1)
    conv_kernel = jnp.concatenate([conv_x, conv_bc], axis=1)
    padded = jnp.concatenate([jnp.zeros((CONV - 1, INNER + 2 * STATE), jnp.float32), raw_input], axis=0)
    seg_padded = jnp.concatenate([jnp.full((CONV - 1,), -1, jnp.int32), seg_ids.astype(jnp.int32)])
    conv_sum = jnp.zeros_like(raw_input)
    for tap_row in range(CONV):
        same_tenant = (seg_padded[tap_row:tap_row + TOKENS] == seg_ids).astype(jnp.float32)
        conv_sum = conv_sum + conv_kernel[tap_row] * padded[tap_row:tap_row + TOKENS] * same_tenant[:, None]
    activated = jax.nn.silu(conv_sum)
    x_heads = activated[:, :INNER].reshape(TOKENS, MHEADS, HEADDIM)
    input_b = activated[:, INNER:INNER + STATE]
    output_c = activated[:, INNER + STATE:]
    begins = (seg_padded[CONV - 2:CONV - 2 + TOKENS] != seg_ids).astype(jnp.float32)
    factor = jnp.exp(-step_size * decay_rate) * (1.0 - begins)[:, None]
    last_rows = tenant_bounds[:, 1] - 1
    positions = jnp.arange(TOKENS, dtype=jnp.int32)

    def advance(carry, item):
        state, saved = carry
        factor_row, step_row, x_row, b_row, c_row, place = item
        state = factor_row[:, None, None] * state + (step_row[:, None] * x_row)[:, :, None] * b_row[None, None, :]
        marks = last_rows == place
        saved = lax.cond(jnp.any(marks), lambda kept: kept + marks.astype(jnp.float32)[:, None, None, None] * state[None], lambda kept: kept, saved)
        return ((state, saved), lax.optimization_barrier(jnp.sum(state * c_row[None, None, :], axis=-1)))
    start_state = jnp.zeros((MHEADS, HEADDIM, STATE), jnp.float32)
    start_saved = jnp.zeros((TENANTS, MHEADS, HEADDIM, STATE), jnp.float32)
    (final_state, tenant_states), y_scan = lax.scan(advance, (start_state, start_saved), (factor, step_size, x_heads, input_b, output_c, positions))
    y_full = y_scan + skip_gain[None, :, None] * x_heads
    gated = y_full.reshape(TOKENS, INNER) * jax.nn.silu(projected[:, INNER:])
    inner_scale = lax.rsqrt(lax.optimization_barrier(jnp.mean(gated * gated, axis=1, keepdims=True)) + 1e-05)
    scaled = (gated * inner_scale * inner_gain).astype(jnp.bfloat16)
    after_mix = (wide + jnp.dot(scaled, w_out, preferred_element_type=jnp.float32)).astype(jnp.bfloat16)
    wide_mix = after_mix.astype(jnp.float32)
    normed_attn = (wide_mix * rms_scale(wide_mix) * attn_gain).astype(jnp.bfloat16)
    qkv_rows = times_rows(normed_attn, w_qkv.reshape(3 * ATT, D)).astype(jnp.bfloat16)
    queries = qkv_rows[:, :ATT].reshape(TOKENS, HEADS, HEAD_SIZE).transpose(1, 0, 2)
    keys = qkv_rows[:, ATT:2 * ATT].reshape(TOKENS, HEADS, HEAD_SIZE).transpose(1, 0, 2)
    values = qkv_rows[:, 2 * ATT:].reshape(TOKENS, HEADS, HEAD_SIZE).transpose(1, 0, 2)
    kv_cache = jnp.stack([qkv_rows[:, ATT:2 * ATT].T, qkv_rows[:, 2 * ATT:].T])
    visible = (seg_ids[:, None] == seg_ids[None, :]) & (positions[None, :] <= positions[:, None]) & (pad_mask[None, :] > 0)
    visible_float = visible.astype(jnp.float32)
    score_scale = 1.0 / math.sqrt(HEAD_SIZE)

    def one_head(operands):
        query_head, key_head, value_head = operands
        scores = jnp.dot(query_head, key_head.T, preferred_element_type=jnp.float32) * score_scale
        scores = jnp.where(visible, scores, -1e+30)
        peak = lax.optimization_barrier(jnp.max(scores, axis=1, keepdims=True))
        weights = jnp.exp(scores - peak) * visible_float
        total = lax.optimization_barrier(jnp.sum(weights, axis=1, keepdims=True))
        context = jnp.dot(weights.astype(jnp.bfloat16), value_head, preferred_element_type=jnp.float32) / total
        return context.astype(jnp.bfloat16)
    contexts = lax.map(one_head, (queries, keys, values))
    context_rows = contexts.transpose(1, 0, 2).reshape(TOKENS, ATT)
    hidden_out = (wide_mix + jnp.dot(context_rows, w_o, preferred_element_type=jnp.float32)).astype(jnp.bfloat16)
    return (hidden_out, kv_cache, tenant_states)
```

```python
import functools

import jax
import jax.numpy as jnp
import numpy as np
from jax import lax
from jax.experimental import pallas as pl
from jax.experimental.pallas import tpu as pltpu
from jax.sharding import PartitionSpec as P

F32 = jnp.float32
BF16 = jnp.bfloat16
EPS = 1e-05
NEG = -1e30


def ring_order(count):
    columns = {8: 2, 32: 4}.get(count, 0)
    if not columns:
        return list(range(count))
    rows = count // columns
    order = [row * columns for row in range(rows)]
    for row in reversed(range(rows)):
        inner = list(range(1, columns))
        if (rows - 1 - row) % 2:
            inner.reverse()
        order += [row * columns + column for column in inner]
    return order


def sources(count):
    order = ring_order(count)
    place = {device: i for i, device in enumerate(order)}
    table = np.zeros((count, count), np.int32)
    for device in range(count):
        at = place[device]
        slots = [order[at]]
        for hop in range(1, (count - 1) // 2 + 1):
            slots += [order[(at - hop) % count], order[(at + hop) % count]]
        if count % 2 == 0 and count > 1:
            slots.append(order[(at + count // 2) % count])
        table[device] = slots
    return table


def ring_gather(piece, axis, count):
    order = ring_order(count)
    ahead = [(order[i], order[(i + 1) % count]) for i in range(count)]
    behind = [(order[i], order[(i - 1) % count]) for i in range(count)]
    pieces = [piece]
    one = two = piece
    for _ in range((count - 1) // 2):
        one = lax.ppermute(one, axis, ahead)
        two = lax.ppermute(two, axis, behind)
        pieces += [one, two]
    if count % 2 == 0 and count > 1:
        half = piece.shape[0] // 2
        if half % 16 == 0:
            one = lax.ppermute(one[:half], axis, ahead)
            two = lax.ppermute(two[half:], axis, behind)
            pieces += [one, two]
        else:
            pieces.append(lax.ppermute(one, axis, ahead))
    return pieces


def lay_out(slots_ref, piece_refs, rows, full_ref):
    columns = full_ref.shape[1]
    total = jnp.zeros((8, columns), F32)
    slot = 0
    done = 0
    for piece in piece_refs:
        count = piece.shape[0]
        strip = next(s for s in (64, 32, 16, 8) if count % s == 0)
        start = slots_ref[slot] * rows + done

        def body(i, carry, piece=piece, strip=strip, start=start):
            part = piece[pl.ds(pl.multiple_of(i * strip, strip), strip), :]
            full_ref[pl.ds(pl.multiple_of(start + i * strip, 16), strip), :] = part
            wide = part.astype(F32)
            return carry + jnp.sum((wide * wide).reshape(strip // 8, 8, columns), axis=0)

        total = lax.fori_loop(0, count // strip, body, total)
        done += count
        if done == rows:
            slot, done = slot + 1, 0
    return jnp.sum(total, axis=0, keepdims=True)


def call(kernel, out_shape, operands, smem=(), scratch=(), flops=0):
    specs = [
        pl.BlockSpec(memory_space=pltpu.SMEM if i in smem else pltpu.VMEM)
        for i in range(len(operands))
    ]
    size = sum(o.size * o.dtype.itemsize for o in operands)
    return pl.pallas_call(
        kernel,
        out_shape=out_shape,
        in_specs=specs,
        out_specs=jax.tree.map(lambda _: pl.BlockSpec(memory_space=pltpu.VMEM), out_shape),
        scratch_shapes=list(scratch),
        compiler_params=pltpu.CompilerParams(vmem_limit_bytes=40 << 20),
        cost_estimate=pl.CostEstimate(flops=flops, bytes_accessed=size, transcendentals=0),
    )(*operands)


def silu(value):
    return value / (1.0 + jnp.exp(-value))


def in_kernel(pieces, rows, conv_rows, inner, *refs):
    slots_ref = refs[0]
    piece_refs = refs[1 : 1 + pieces]
    w_ref, raw_ref, z_ref, dt_ref, tail_ref, full_ref, acc_ref = refs[1 + pieces :]
    width = full_ref.shape[0]
    squares = lay_out(slots_ref, piece_refs, rows, full_ref)
    scale = lax.rsqrt(squares / width + EPS)
    acc_ref[...] = jnp.dot(w_ref[...], full_ref[...], preferred_element_type=F32)
    raw_ref[...] = acc_ref[:conv_rows, :] * scale
    z_ref[...] = acc_ref[conv_rows : conv_rows + inner, :] * scale
    dt_ref[...] = acc_ref[conv_rows + inner :, :] * scale
    last = raw_ref.shape[1] - 128
    tail_ref[...] = raw_ref[:, last:].T[120:, :]


def mix_kernel(
    tenants,
    heads,
    scal_ref,
    raw_ref,
    dt_ref,
    halo_ref,
    taps_ref,
    head_ref,
    rel_ref,
    live_ref,
    pad_ref,
    y_ref,
    c_ref,
    entry_ref,
    pay_ref,
    local_ref,
    ext_ref,
    x_ref,
    xdt_ref,
):
    conv_rows, toks = raw_ref.shape
    inner = y_ref.shape[0]
    hd = inner // heads
    rel = rel_ref[...]
    lane = lax.broadcasted_iota(jnp.int32, (1, toks), 1)
    before = jnp.concatenate([jnp.zeros((120, conv_rows), F32), halo_ref[...]], axis=0).T
    ext_ref[:, :128] = before
    ext_ref[:, 128:] = raw_ref[...]
    strip = 64
    keep = [(rel >= shift).astype(F32) for shift in range(4)]
    for i in range(conv_rows // strip):
        rows = pl.ds(i * strip, strip)
        ext = ext_ref[rows, :]
        taps = taps_ref[rows, :]
        total = taps[:, 3:4] * ext[:, 128:]
        for shift in range(1, 4):
            moved = pltpu.roll(ext, shift, 1)[:, 128:]
            total = total + taps[:, 3 - shift : 4 - shift] * moved * keep[shift]
        x_ref[rows, :] = silu(total)
    step = dt_ref[...] + head_ref[:, 0:1]
    step = (jnp.maximum(step, 0.0) + jnp.log1p(jnp.exp(-jnp.abs(step)))) * live_ref[...]
    logs = -step * head_ref[:, 1:2]
    shift = 1
    while shift < toks:
        logs = logs + jnp.where(lane >= shift, pltpu.roll(logs, shift, 1), 0.0)
        shift *= 2
    start = lane - rel
    entry_ref[...] = jnp.exp(logs) * (start < 0).astype(F32)
    for h in range(heads):
        xdt_ref[h * hd : (h + 1) * hd, :] = x_ref[h * hd : (h + 1) * hd, :] * step[h : h + 1, :]
    input_b = x_ref[inner : inner + 64, :]
    output_c = x_ref[inner + 64 : inner + 128, :].astype(BF16)
    c_ref[...] = output_c
    bc_tok = x_ref[inner : inner + 128, :].T
    b_tok = bc_tok[:, :64].astype(BF16)
    columns = [
        jnp.broadcast_to(logs[h : h + 1, :], (128, toks)).T for h in range(heads)
    ]
    for block in range(toks // 128):
        here = slice(block * 128, (block + 1) * 128)
        upto = (block + 1) * 128
        key = lax.broadcasted_iota(jnp.int32, (upto, 128), 0)
        seen = (key <= lane[:, here]) & (key >= start[:, here])
        bias = jnp.where(seen, 0.0, NEG)
        c_dot_b = jnp.dot(b_tok[:upto, :], output_c[:, here], preferred_element_type=F32)
        for h in range(heads):
            gap = logs[h : h + 1, here] - columns[h][:upto, :]
            mixing = (jnp.exp(jnp.minimum(gap, 0.0) + bias) * c_dot_b).astype(BF16)
            rows = slice(h * hd, (h + 1) * hd)
            y_ref[rows, here] = (
                jnp.dot(
                    xdt_ref[rows, :upto].astype(BF16), mixing, preferred_element_type=F32
                )
                + head_ref[h : h + 1, 2:3] * x_ref[rows, here]
            )
    wide_b = bc_tok.astype(BF16)
    tok = lax.broadcasted_iota(jnp.int32, (inner, 128), 1)
    for k in range(tenants + 1):
        pick, first = scal_ref[k], scal_ref[8 + k]
        at = jnp.sum(jnp.where(lane == pick, logs, 0.0), axis=1, keepdims=True)
        inside = (lane <= pick) & (lane >= first)
        toward = jnp.exp(jnp.minimum(at - logs, 0.0) + jnp.where(inside, 0.0, NEG))
        carried = jnp.exp(at) * jnp.where(first < 0, 1.0, 0.0)
        lhs = jnp.concatenate(
            [
                (xdt_ref[h * hd : (h + 1) * hd, :] * toward[h : h + 1, :]).astype(BF16)
                for h in range(heads)
            ],
            axis=0,
        )
        state = jnp.dot(lhs, wide_b, preferred_element_type=F32)
        factor = jnp.concatenate(
            [jnp.broadcast_to(carried[h : h + 1, :], (hd, 128)) for h in range(heads)], axis=0
        )
        if k < tenants:
            local_ref[k * inner : (k + 1) * inner, :] = jnp.where(tok < 64, state, factor)
        else:
            high = factor.astype(BF16).astype(F32)
            packed = jnp.where(tok < 64, state, jnp.where(tok < 96, high, factor - high))
            pay_ref[:inner, :] = packed.astype(BF16)
    pay_ref[inner:, :] = pad_ref[...].astype(BF16)


def gate_kernel(tenants, heads, count, *refs):
    scal_ref = refs[0]
    pay_refs = refs[1 : 1 + count]
    y_ref, z_ref, c_ref, entry_ref, local_ref, g_ref, tenant_ref = refs[1 + count :]
    inner = y_ref.shape[0]
    hd = inner // heads
    incoming = jnp.zeros((inner, 64), F32)
    decay = jnp.ones((inner, 1), F32)
    for pay in pay_refs:
        wide = pay[:inner, :].astype(F32)
        incoming = incoming + decay * wide[:, :64]
        decay = decay * (wide[:, 64:65] + wide[:, 96:97])
    for h in range(heads):
        rows = slice(h * hd, (h + 1) * hd)
        carry = jnp.dot(incoming[rows, :].astype(BF16), c_ref[...], preferred_element_type=F32)
        y_full = y_ref[rows, :] + carry * entry_ref[h : h + 1, :]
        g_ref[rows, :] = (y_full * silu(z_ref[rows, :])).astype(BF16)
    for k in range(tenants):
        rows = slice(k * inner, (k + 1) * inner)
        owned = scal_ref[16 + k].astype(F32)
        local = local_ref[rows, :]
        tenant_ref[rows, :] = ((local[:, 64:65] * incoming + local[:, :64]) * owned).astype(BF16)


def mixed_kernel(pieces, rows, *refs):
    slots_ref = refs[0]
    piece_refs = refs[1 : 1 + pieces]
    w_ref, hidden_ref, out_ref, full_ref = refs[1 + pieces :]
    squares = lay_out(slots_ref, piece_refs, rows, full_ref)
    scale = lax.rsqrt(squares / full_ref.shape[0] + EPS)
    product = jnp.dot(w_ref[...], full_ref[...], preferred_element_type=F32)
    out_ref[...] = (hidden_ref[...].astype(F32) + product * scale).astype(BF16)


def qkv_kernel(pieces, rows, *refs):
    slots_ref = refs[0]
    piece_refs = refs[1 : 1 + pieces]
    w_ref, q_ref, kv_ref, full_ref = refs[1 + pieces :]
    squares = lay_out(slots_ref, piece_refs, rows, full_ref)
    scale = lax.rsqrt(squares / full_ref.shape[0] + EPS)
    product = jnp.dot(w_ref[...], full_ref[...], preferred_element_type=F32)
    att = q_ref.shape[0]
    q_ref[...] = (product[:att] * scale).astype(BF16)
    kv_ref[...] = (product[att:] * scale).astype(BF16)


def attend_kernel(blocks, score_scale, *refs):
    scal_ref, q_ref = refs[:2]
    kv_refs = refs[2 : 2 + blocks]
    pad_ref, rel_ref, ctx_ref, q_aug, k_aug, peak_ref, total_ref, sum_ref = refs[2 + blocks :]
    att, toks = q_ref.shape
    extra = q_aug.shape[0] - att
    row = lax.broadcasted_iota(jnp.int32, (extra, toks), 0)
    q_aug[:att, :] = q_ref[...]
    q_aug[att:, :] = jnp.where(row == 0, 1.0, 0.0).astype(BF16)
    place = scal_ref[0] * toks + lax.broadcasted_iota(jnp.int32, (1, toks), 1)
    start = place - rel_ref[...]
    peak_ref[...] = jnp.full(peak_ref.shape, NEG, F32)
    total_ref[...] = jnp.zeros(total_ref.shape, F32)
    sum_ref[...] = jnp.zeros(sum_ref.shape, F32)
    for b in range(blocks):

        @pl.when(scal_ref[32 + b] > 0)
        def _(b=b):
            count = kv_refs[b].shape[1]
            k_aug[:att, :] = kv_refs[b][:att, :]
            bias = (pad_ref[b : b + 1, :] - 1.0) * 1e30
            k_aug[att:, :] = jnp.where(row == 0, bias, 0.0).astype(BF16)
            scores = (
                lax.dot_general(
                    k_aug[...], q_aug[...], (((0,), (0,)), ((), ())), preferred_element_type=F32
                )
                * score_scale
            )
            key = scal_ref[16 + b] * count + lax.broadcasted_iota(jnp.int32, (count, toks), 0)
            scores = jnp.where((key <= place) & (key >= start), scores, NEG)
            peak = jnp.maximum(peak_ref[...], jnp.max(scores, axis=0, keepdims=True))
            weights = jnp.exp(scores - peak)
            keep = jnp.exp(peak_ref[...] - peak)
            peak_ref[...] = peak
            total_ref[...] = total_ref[...] * keep + jnp.sum(weights, axis=0, keepdims=True)
            sum_ref[...] = sum_ref[...] * keep + jnp.dot(
                kv_refs[b][att:, :], weights.astype(BF16), preferred_element_type=F32
            )

    ctx_ref[...] = (sum_ref[...] / total_ref[...]).astype(BF16)


def last_kernel(pieces, rows, *refs):
    slots_ref = refs[0]
    piece_refs = refs[1 : 1 + pieces]
    w_ref, mixed_ref, out_ref, full_ref = refs[1 + pieces :]
    lay_out(slots_ref, piece_refs, rows, full_ref)
    product = jnp.dot(w_ref[...], full_ref[...], preferred_element_type=F32)
    out_ref[...] = (mixed_ref[...].astype(F32) + product).T.astype(BF16)


def on_device(
    tp_count,
    seq_count,
    hidden_in,
    mamba_gain,
    w_xz,
    w_bc,
    w_dt,
    dt_bias,
    decay_rate,
    conv_x,
    conv_bc,
    skip_gain,
    inner_gain,
    w_out,
    attn_gain,
    w_qkv,
    w_o,
    seg_ids,
    pad_mask,
    tenant_bounds,
):
    toks, part = hidden_in.shape
    width = mamba_gain.shape[0]
    inner = w_xz.shape[1]
    heads = decay_rate.shape[0]
    att = w_qkv.shape[1]
    tenants = tenant_bounds.shape[0]
    bc = w_bc.shape[1]
    conv_rows = inner + bc
    seq = lax.axis_index("seq")
    tp = lax.axis_index("tp")
    sds = jax.ShapeDtypeStruct

    hidden_t = hidden_in.T
    full_in = ring_gather(hidden_t, "tp", tp_count)
    pieces = len(full_in)
    slots = jnp.asarray(sources(tp_count))[tp]

    seq_base = seq * toks
    run_starts, run_ends = tenant_bounds[:, 0], tenant_bounds[:, 1]
    places = seq_base + jnp.arange(toks, dtype=jnp.int32)
    tenant_ids = jnp.arange(tenants, dtype=jnp.int32)
    my_start = jnp.sum(
        jnp.where(seg_ids[:, None] == tenant_ids[None, :], run_starts[None, :], 0), axis=1
    )
    rel = (places - my_start)[None, :]
    live = pad_mask.astype(F32)[None, :]
    pad_block = jnp.pad(pad_mask.astype(F32).reshape(toks // 128, 128), ((0, 16 - toks // 128), (0, 0)))
    picks = jnp.concatenate(
        [jnp.clip(run_ends - 1 - seq_base, 0, toks - 1), jnp.full((1,), toks - 1, jnp.int32)]
    )
    firsts = jnp.concatenate([run_starts, my_start[-1:]]) - seq_base
    owned = ((run_ends - 1 >= seq_base) & (run_ends - 1 < seq_base + toks)).astype(jnp.int32)
    scal = jnp.concatenate(
        [
            jnp.pad(picks, (0, 8 - tenants - 1)),
            jnp.pad(firsts, (0, 8 - tenants - 1)),
            jnp.pad(owned, (0, 8 - tenants)),
        ]
    )
    head_table = jnp.pad(
        jnp.stack([dt_bias, decay_rate, skip_gain], axis=1), ((0, 8 - heads), (0, 128 - 3))
    )
    taps = jnp.pad(jnp.concatenate([conv_x, conv_bc], axis=1).T, ((0, 0), (0, 124)))

    w_in = (
        jnp.concatenate([w_xz[0], w_bc.T, w_xz[1], jnp.pad(w_dt, ((0, 8 - heads), (0, 0)))], axis=0)
        .astype(F32)
        * mamba_gain
    ).astype(BF16)
    w_att = (w_qkv.reshape(3 * att, width).astype(F32) * attn_gain).astype(BF16)

    w_rows = jnp.concatenate([(w_out.astype(F32) * inner_gain[:, None]).astype(BF16), w_o], axis=0)
    share = w_rows.shape[0] // seq_count
    mine = lax.dynamic_slice_in_dim(w_rows, seq * share, share, axis=0)
    mine = mine.reshape(share, tp_count, part).transpose(1, 0, 2)
    swapped = lax.all_to_all(mine, "tp", 0, 0, tiled=False)
    w_cols = lax.all_gather(swapped, "seq", axis=0, tiled=False)
    w_cols = w_cols.transpose(1, 0, 2, 3).reshape(tp_count, inner + att, part)
    w_out_t = w_cols[:, :inner].reshape(tp_count * inner, part).T
    w_o_t = w_cols[:, inner:].reshape(tp_count * att, part).T

    in_rows = conv_rows + inner + 8
    raw, z, dt_raw, tail = call(
        functools.partial(in_kernel, pieces, part, conv_rows, inner),
        (
            sds((conv_rows, toks), F32),
            sds((inner, toks), F32),
            sds((8, toks), F32),
            sds((8, conv_rows), F32),
        ),
        (slots, *full_in, w_in),
        smem=(0,),
        scratch=[pltpu.VMEM((width, toks), BF16), pltpu.VMEM((in_rows, toks), F32)],
        flops=2 * in_rows * width * toks,
    )
    halo = lax.ppermute(tail, "seq", [(i, i + 1) for i in range(seq_count - 1)])
    y, c_rows, entry, pay, local = call(
        functools.partial(mix_kernel, tenants, heads),
        (
            sds((inner, toks), F32),
            sds((bc // 2, toks), BF16),
            sds((8, toks), F32),
            sds((inner + 16, 128), BF16),
            sds((tenants * inner, 128), F32),
        ),
        (scal, raw, dt_raw, halo, taps, head_table, rel, live, pad_block),
        smem=(0,),
        scratch=[
            pltpu.VMEM((conv_rows, toks + 128), F32),
            pltpu.VMEM((conv_rows, toks), F32),
            pltpu.VMEM((inner, toks), F32),
        ],
        flops=10**9,
    )
    pays = [
        lax.ppermute(pay, "seq", [(i, i + by) for i in range(seq_count - by)])
        for by in range(1, seq_count)
    ]
    gated, tenant_part = call(
        functools.partial(gate_kernel, tenants, heads, len(pays)),
        (sds((inner, toks), BF16), sds((tenants * inner, bc // 2), BF16)),
        (scal, *pays, y, z, c_rows, entry, local),
        smem=(0,),
        flops=10**8,
    )
    tenant_states = (
        lax.psum(tenant_part, "seq")
        .astype(F32)
        .reshape(tenants, heads, inner // heads, bc // 2)
    )
    full_gated = ring_gather(gated, "tp", tp_count)
    mixed = call(
        functools.partial(mixed_kernel, len(full_gated), inner),
        sds((part, toks), BF16),
        (slots, *full_gated, w_out_t, hidden_t),
        smem=(0,),
        scratch=[pltpu.VMEM((tp_count * inner, toks), BF16)],
        flops=2 * part * tp_count * inner * toks,
    )
    full_mixed = ring_gather(mixed, "tp", tp_count)
    queries, kv = call(
        functools.partial(qkv_kernel, len(full_mixed), part),
        (sds((att, toks), BF16), sds((2 * att, toks), BF16)),
        (slots, *full_mixed, w_att),
        smem=(0,),
        scratch=[pltpu.VMEM((width, toks), BF16)],
        flops=6 * att * width * toks,
    )
    kv_cache = kv.reshape(2, att, toks)

    def pad_row(block):
        return block[inner : inner + toks // 128].astype(F32).reshape(1, toks)

    if seq_count == 4:
        near = lax.ppermute(kv, "seq", [(0, 1), (2, 3)])
        far = lax.ppermute(kv, "seq", [(0, 2), (1, 3)])
        other = lax.ppermute(far, "seq", [(2, 3), (3, 2)])
        buffers = [kv, near, far, other]
        odd = seq % 2
        block_ids = jnp.stack([seq, seq - 1 + 2 * (1 - odd), seq - 2, seq - 1 - 2 * odd])
        rows = [pad_row(p) for p in pays]
        pads = [live, rows[0], rows[1], jnp.where(odd > 0, rows[2], rows[0])]
    else:
        gathered = lax.all_gather(kv, "seq", axis=0, tiled=False)
        buffers = [gathered[i] for i in range(seq_count)]
        block_ids = jnp.arange(seq_count, dtype=jnp.int32)
        all_pads = lax.all_gather(live, "seq", axis=0, tiled=True)
        pads = [all_pads[i : i + 1] for i in range(seq_count)]
    blocks = len(buffers)
    pads = jnp.concatenate(pads, axis=0)
    wanted = (
        (block_ids >= 0) & (block_ids <= seq) & (block_ids * toks + toks > my_start[0])
    ).astype(jnp.int32)
    att_scal = jnp.concatenate(
        [
            jnp.full((16,), seq, jnp.int32),
            jnp.pad(block_ids.astype(jnp.int32), (0, 16 - blocks)),
            jnp.pad(wanted, (0, 16 - blocks)),
        ]
    )
    deep = att + 32
    context = call(
        functools.partial(attend_kernel, blocks, att ** (-0.5)),
        sds((att, toks), BF16),
        (att_scal, queries, *buffers, pads, rel),
        smem=(0,),
        scratch=[
            pltpu.VMEM((deep, toks), BF16),
            pltpu.VMEM((deep, toks), BF16),
            pltpu.VMEM((1, toks), F32),
            pltpu.VMEM((1, toks), F32),
            pltpu.VMEM((att, toks), F32),
        ],
        flops=4 * blocks * toks * toks * att,
    )
    full_context = ring_gather(context, "tp", tp_count)
    hidden_out = call(
        functools.partial(last_kernel, len(full_context), att),
        sds((toks, part), BF16),
        (slots, *full_context, w_o_t, mixed),
        smem=(0,),
        scratch=[pltpu.VMEM((tp_count * att, toks), BF16)],
        flops=2 * part * tp_count * att * toks,
    )
    return (hidden_out, kv_cache, tenant_states)


def solution(mesh):
    return jax.shard_map(
        functools.partial(on_device, mesh.shape["tp"], mesh.shape["seq"]),
        mesh=mesh,
        in_specs=(
            P("seq", "tp"),
            P(),
            P(None, "tp", None),
            P(),
            P("tp", None),
            P("tp"),
            P("tp"),
            P(None, "tp"),
            P(),
            P("tp"),
            P("tp"),
            P("tp", None),
            P(),
            P(None, "tp", None),
            P("tp", None),
            P("seq"),
            P("seq"),
            P(),
        ),
        out_specs=(P("seq", "tp"), P(None, "tp", "seq"), P(None, "tp", None, None)),
        check_vma=False,
    )
```

```python
import functools

import jax
import jax.numpy as jnp
import numpy as np
from jax import lax
from jax.experimental import pallas as pl
from jax.experimental.pallas import tpu as pltpu
from jax.sharding import PartitionSpec as P

F32 = jnp.float32
BF16 = jnp.bfloat16
EPS = 1e-05
NEG = -1e30


def ring_order(count):
    columns = {8: 2, 32: 4}.get(count, 0)
    if not columns:
        return list(range(count))
    rows = count // columns
    order = [row * columns for row in range(rows)]
    for row in reversed(range(rows)):
        inner = list(range(1, columns))
        if (rows - 1 - row) % 2:
            inner.reverse()
        order += [row * columns + column for column in inner]
    return order


def sources(count):
    order = ring_order(count)
    place = {device: i for i, device in enumerate(order)}
    table = np.zeros((count, count), np.int32)
    for device in range(count):
        at = place[device]
        slots = [order[at]]
        for hop in range(1, (count - 1) // 2 + 1):
            slots += [order[(at - hop) % count], order[(at + hop) % count]]
        if count % 2 == 0 and count > 1:
            slots.append(order[(at + count // 2) % count])
        table[device] = slots
    return table


def ring_gather(piece, axis, count, split=False, tasks=()):
    order = ring_order(count)
    ahead = [(order[i], order[(i + 1) % count]) for i in range(count)]
    behind = [(order[i], order[(i - 1) % count]) for i in range(count)]
    half = piece.shape[0] // 2
    split = split and half % 16 == 0
    parts = [piece[:half], piece[half:]] if split else [piece]
    far_hop = (count - 1) // 2 + 1
    last_hop = far_hop if count % 2 == 0 else far_hop - 1
    here = {(0, i): (part, part) for i, part in enumerate(parts)}
    results = [None] * len(tasks)
    finished = [(piece,)]
    step = 0
    for hop in range(1, last_hop + 1):
        for i in range(len(parts)):
            one, two = here[hop - 1, i]
            wait = finished[max(0, len(finished) - 3)] if split else finished[-1]
            ends = [t for t, task in enumerate(tasks) if task[1] == step - 1]
            held = [results[t] for t in ends]
            one, two, _, held = lax.optimization_barrier((one, two, wait, held))
            for t, value in zip(ends, held, strict=True):
                results[t] = value
            if hop < far_hop:
                got = (lax.ppermute(one, axis, ahead), lax.ppermute(two, axis, behind))
            elif not split and half % 16 == 0:
                got = (lax.ppermute(one[:half], axis, ahead), lax.ppermute(two[half:], axis, behind))
            elif i == 0:
                got = (lax.ppermute(one, axis, ahead),) * 2
            else:
                got = (lax.ppermute(two, axis, behind),) * 2
            here[hop, i] = got
            for t, task in enumerate(tasks):
                if task[0] == step:
                    recent = finished[max(0, step + 1 - len(parts)) :]
                    results[t] = task[2]([value for pair in recent for value in pair])
            finished.append(got)
            step += 1
    pieces = [piece]
    for hop in range(1, last_hop + 1):
        if hop < far_hop:
            for side in range(2):
                pieces += [here[hop, i][side] for i in range(len(parts))]
        elif not split and half % 16 == 0:
            pieces += list(here[hop, 0])
        else:
            pieces += [here[hop, i][0] for i in range(len(parts))]
    return pieces, results


def sum_pairs(value, axis, count):
    by = 1
    while by < count:
        value = value + lax.ppermute(value, axis, [(i, i ^ by) for i in range(count)])
        by *= 2
    return value


def lay_out(slots_ref, piece_refs, rows, full_ref):
    columns = full_ref.shape[1]
    total = jnp.zeros((8, columns), F32)
    slot = 0
    done = 0
    for piece in piece_refs:
        count = piece.shape[0]
        strip = next(s for s in (64, 32, 16, 8) if count % s == 0)
        start = slots_ref[lax.axis_index("tp"), slot] * rows + done

        def body(i, carry, piece=piece, strip=strip, start=start):
            part = piece[pl.ds(pl.multiple_of(i * strip, strip), strip), :]
            full_ref[pl.ds(pl.multiple_of(start + i * strip, 16), strip), :] = part
            wide = part.astype(F32)
            return carry + jnp.sum((wide * wide).reshape(strip // 8, 8, columns), axis=0)

        total = lax.fori_loop(0, count // strip, body, total)
        done += count
        if done == rows:
            slot, done = slot + 1, 0
    return jnp.sum(total, axis=0, keepdims=True)


def call(kernel, out_shape, operands, smem=(), scratch=(), flops=0, vmem=12):
    specs = [
        pl.BlockSpec(
            memory_space=pltpu.SMEM if i in smem else pltpu.VMEM
        )
        for i in range(len(operands))
    ]
    size = sum(o.size * o.dtype.itemsize for o in operands)
    return pl.pallas_call(
        kernel,
        out_shape=out_shape,
        in_specs=specs,
        out_specs=jax.tree.map(lambda _: pl.BlockSpec(memory_space=pltpu.VMEM), out_shape),
        scratch_shapes=list(scratch),
        compiler_params=pltpu.CompilerParams(vmem_limit_bytes=vmem << 20),
        cost_estimate=pl.CostEstimate(flops=flops, bytes_accessed=size, transcendentals=0),
    )(*operands)


def after(values, first):
    return lax.optimization_barrier((*values, first))


def silu(value):
    return value / (1.0 + jnp.exp(-value))


def share_kernel(seq_ref, out_ref, o_ref, gain_ref, mine_ref, mine_o_ref):
    count, part = mine_ref.shape[0], mine_ref.shape[2]
    for d in range(count):
        columns = slice(d * part, (d + 1) * part)
        scaled = out_ref[:, columns].astype(F32) * gain_ref[:, 0:1]
        mine_ref[d, :, :] = scaled.astype(BF16)
        mine_o_ref[d, :, :] = o_ref[:, columns]


def weights_kernel(xz_ref, bc_ref, dt_ref, gain_ref, w_ref):
    inner = xz_ref.shape[1]
    bc = bc_ref.shape[1]
    width = gain_ref.shape[1]
    tile = 512
    for i in range(width // tile):
        at = slice(i * tile, (i + 1) * tile)
        gain = gain_ref[:, at]

        def put(first, value, at=at, gain=gain):
            w_ref[first : first + value.shape[0], at] = (value.astype(F32) * gain).astype(BF16)

        put(0, xz_ref[0, :, at])
        put(inner, bc_ref[at, :].astype(F32).T)
        put(inner + bc, xz_ref[1, :, at])
        heads = dt_ref.shape[0]
        last = jnp.concatenate(
            [dt_ref[:, at].astype(F32), jnp.zeros((16 - heads, tile), F32)], axis=0
        )
        put(2 * inner + bc, last)


def run_starts(seg_ref, bounds_ref):
    seg = seg_ref[...]
    start = jnp.zeros(seg.shape, jnp.int32)
    for t in range(bounds_ref.shape[0]):
        start = jnp.where(seg == t, bounds_ref[t, 0], start)
    return start


def start_at(place, bounds_ref):
    start = jnp.int32(0)
    for t in range(bounds_ref.shape[0]):
        start = jnp.where(place >= bounds_ref[t, 0], bounds_ref[t, 0], start)
    return start


def turn_kernel(cols_ref, out_ref):
    rows = cols_ref.shape[0]
    tile = 256 if rows % 256 == 0 else rows
    for i in range(rows // tile):
        at = slice(i * tile, (i + 1) * tile)
        out_ref[:, at] = cols_ref[at, :].astype(F32).T.astype(BF16)


def in_kernel(pieces, rows, conv_rows, inner, *refs):
    slots_ref = refs[0]
    piece_refs = refs[1 : 1 + pieces]
    w_ref, raw_ref, z_ref, dt_ref, tail_ref, full_ref, acc_ref = refs[1 + pieces :]
    squares = lay_out(slots_ref, piece_refs, rows, full_ref)
    scale = lax.rsqrt(squares / full_ref.shape[0] + EPS)
    acc_ref[...] = jnp.dot(w_ref[...], full_ref[...], preferred_element_type=F32)
    raw_ref[...] = acc_ref[:conv_rows, :] * scale
    z_ref[...] = acc_ref[conv_rows : conv_rows + inner, :] * scale
    dt_ref[...] = acc_ref[conv_rows + inner : conv_rows + inner + 8, :] * scale
    last = raw_ref.shape[1] - 128
    tail_ref[...] = raw_ref[:, last:].T[120:, :]


def mix_kernel(
    tenants,
    heads,
    bounds_ref,
    bias_ref,
    rate_ref,
    skip_ref,
    raw_ref,
    dt_ref,
    halo_ref,
    conv_x_ref,
    conv_bc_ref,
    seg_ref,
    live_ref,
    y_ref,
    c_ref,
    entry_ref,
    pay_ref,
    local_ref,
    ext_ref,
    x_ref,
    xdt_ref,
    taps_ref,
):
    conv_rows, toks = raw_ref.shape
    inner = y_ref.shape[0]
    hd = inner // heads
    lane = lax.broadcasted_iota(jnp.int32, (1, toks), 1)
    base = lax.axis_index("seq") * toks
    rel = base + lane - run_starts(seg_ref, bounds_ref)
    live = live_ref[...].astype(F32)
    count = conv_x_ref.shape[0]
    both = jnp.concatenate([conv_x_ref[...], conv_bc_ref[...]], axis=1)
    taps_ref[...] = jnp.concatenate([both, jnp.zeros((128 - count, conv_rows), F32)], axis=0).T
    head = lax.broadcasted_iota(jnp.int32, (8, 1), 0)
    bias = rate = jnp.zeros((8, 1), F32)
    for h in range(heads):
        bias = jnp.where(head == h, bias_ref[h], bias)
        rate = jnp.where(head == h, rate_ref[h], rate)
    before = jnp.concatenate([jnp.zeros((120, conv_rows), F32), halo_ref[...]], axis=0).T
    ext_ref[:, :128] = before
    ext_ref[:, 128:] = raw_ref[...]
    strip = 64
    keep = [(rel >= shift).astype(F32) for shift in range(4)]
    for i in range(conv_rows // strip):
        rows = pl.ds(i * strip, strip)
        ext = ext_ref[rows, :]
        taps = taps_ref[rows, :]
        total = taps[:, 3:4] * ext[:, 128:]
        for shift in range(1, 4):
            moved = pltpu.roll(ext, shift, 1)[:, 128:]
            total = total + taps[:, 3 - shift : 4 - shift] * moved * keep[shift]
        x_ref[rows, :] = silu(total)
    step = dt_ref[...] + bias
    step = (jnp.maximum(step, 0.0) + jnp.log1p(jnp.exp(-jnp.abs(step)))) * live
    logs = -step * rate
    shift = 1
    while shift < toks:
        logs = logs + jnp.where(lane >= shift, pltpu.roll(logs, shift, 1), 0.0)
        shift *= 2
    start = lane - rel
    entry_ref[...] = jnp.exp(logs) * (start < 0).astype(F32)
    for h in range(heads):
        xdt_ref[h * hd : (h + 1) * hd, :] = x_ref[h * hd : (h + 1) * hd, :] * step[h : h + 1, :]
    input_b = x_ref[inner : inner + 64, :]
    output_c = x_ref[inner + 64 : inner + 128, :].astype(BF16)
    c_ref[...] = output_c
    bc_tok = x_ref[inner : inner + 128, :].T
    b_tok = bc_tok[:, :64].astype(BF16)
    columns = [
        jnp.broadcast_to(logs[h : h + 1, :], (128, toks)).T for h in range(heads)
    ]
    for block in range(toks // 128):
        here = slice(block * 128, (block + 1) * 128)
        upto = (block + 1) * 128
        key = lax.broadcasted_iota(jnp.int32, (upto, 128), 0)
        seen = (key <= lane[:, here]) & (key >= start[:, here])
        bias = jnp.where(seen, 0.0, NEG)
        c_dot_b = jnp.dot(b_tok[:upto, :], output_c[:, here], preferred_element_type=F32)
        for h in range(heads):
            gap = logs[h : h + 1, here] - columns[h][:upto, :]
            mixing = (jnp.exp(jnp.minimum(gap, 0.0) + bias) * c_dot_b).astype(BF16)
            rows = slice(h * hd, (h + 1) * hd)
            y_ref[rows, here] = (
                jnp.dot(
                    xdt_ref[rows, :upto].astype(BF16), mixing, preferred_element_type=F32
                )
                + skip_ref[h] * x_ref[rows, here]
            )
    wide_b = bc_tok.astype(BF16)
    tok = lax.broadcasted_iota(jnp.int32, (inner, 128), 1)
    for k in range(tenants + 1):
        if k < tenants:
            pick = jnp.clip(bounds_ref[k, 1] - 1 - base, 0, toks - 1)
            first = bounds_ref[k, 0] - base
        else:
            pick = toks - 1
            first = start_at(base + toks - 1, bounds_ref) - base
        at = jnp.sum(jnp.where(lane == pick, logs, 0.0), axis=1, keepdims=True)
        inside = (lane <= pick) & (lane >= first)
        toward = jnp.exp(jnp.minimum(at - logs, 0.0) + jnp.where(inside, 0.0, NEG))
        carried = jnp.exp(at) * jnp.where(first < 0, 1.0, 0.0)
        lhs = jnp.concatenate(
            [
                (xdt_ref[h * hd : (h + 1) * hd, :] * toward[h : h + 1, :]).astype(BF16)
                for h in range(heads)
            ],
            axis=0,
        )
        state = jnp.dot(lhs, wide_b, preferred_element_type=F32)
        factor = jnp.concatenate(
            [jnp.broadcast_to(carried[h : h + 1, :], (hd, 128)) for h in range(heads)], axis=0
        )
        if k < tenants:
            local_ref[k * inner : (k + 1) * inner, :] = jnp.where(tok < 64, state, factor)
        else:
            high = factor.astype(BF16).astype(F32)
            packed = jnp.where(tok < 64, state, jnp.where(tok < 96, high, factor - high))
            pay_ref[:inner, :] = packed.astype(BF16)
    rows = [live[:, i * 128 : (i + 1) * 128] for i in range(toks // 128)]
    rows.append(jnp.zeros((16 - toks // 128, 128), F32))
    pay_ref[inner:, :] = jnp.concatenate(rows, axis=0).astype(BF16)


def gate_kernel(
    tenants,
    heads,
    bounds_ref,
    pay_ref,
    y_ref,
    z_ref,
    c_ref,
    entry_ref,
    local_ref,
    g_ref,
    tenant_ref,
):
    inner = y_ref.shape[0]
    hd = inner // heads
    incoming = jnp.zeros((inner, 64), F32)
    for block in range(pay_ref.shape[0] - 1):
        wide = pay_ref[block, :inner, :].astype(F32)
        passed = (wide[:, 64:65] + wide[:, 96:97]) * incoming + wide[:, :64]
        incoming = jnp.where(block < lax.axis_index("seq"), passed, incoming)
    for h in range(heads):
        rows = slice(h * hd, (h + 1) * hd)
        carry = jnp.dot(incoming[rows, :].astype(BF16), c_ref[...], preferred_element_type=F32)
        y_full = y_ref[rows, :] + carry * entry_ref[h : h + 1, :]
        g_ref[rows, :] = (y_full * silu(z_ref[rows, :])).astype(BF16)
    for k in range(tenants):
        rows = slice(k * inner, (k + 1) * inner)
        last = bounds_ref[k, 1] - 1 - lax.axis_index("seq") * y_ref.shape[1]
        owned = jnp.where((last >= 0) & (last < y_ref.shape[1]), 1.0, 0.0)
        local = local_ref[rows, :]
        tenant_ref[rows, :] = ((local[:, 64:65] * incoming + local[:, :64]) * owned).astype(BF16)


def mixed_kernel(pieces, rows, *refs):
    slots_ref = refs[0]
    piece_refs = refs[1 : 1 + pieces]
    w_ref, hidden_ref, out_ref, full_ref = refs[1 + pieces :]
    squares = lay_out(slots_ref, piece_refs, rows, full_ref)
    scale = lax.rsqrt(squares / full_ref.shape[0] + EPS)
    product = jnp.dot(w_ref[...], full_ref[...], preferred_element_type=F32)
    out_ref[...] = (hidden_ref[...].astype(F32) + product * scale).astype(BF16)


def qkv_kernel(pieces, rows, *refs):
    slots_ref = refs[0]
    piece_refs = refs[1 : 1 + pieces]
    w_ref, q_ref, k_ref, v_ref, kv_ref, full_ref = refs[1 + pieces :]
    squares = lay_out(slots_ref, piece_refs, rows, full_ref)
    scale = lax.rsqrt(squares / full_ref.shape[0] + EPS)
    product = jnp.dot(w_ref[...], full_ref[...], preferred_element_type=F32)
    att = q_ref.shape[0]
    q_ref[...] = (product[:att] * scale).astype(BF16)
    keys = (product[att : 2 * att] * scale).astype(BF16)
    values = (product[2 * att :] * scale).astype(BF16)
    k_ref[...] = keys
    v_ref[...] = values
    kv_ref[:att, :] = keys
    kv_ref[att:, :] = values


def attend_kernel(blocks, block_of, score_scale, *refs):
    bounds_ref, q_ref = refs[:2]
    k_refs = refs[2 : 2 + blocks]
    v_refs = refs[2 + blocks : 2 + 2 * blocks]
    pay_ref, seg_ref, ctx_ref, q_aug, k_aug, peak_ref, total_ref, sum_ref = refs[2 + 2 * blocks :]
    inner = pay_ref.shape[1] - 16
    seq = lax.axis_index("seq")
    att, toks = q_ref.shape
    extra = q_aug.shape[0] - att
    row = lax.broadcasted_iota(jnp.int32, (extra, toks), 0)
    q_aug[:att, :] = q_ref[...]
    q_aug[att:, :] = jnp.where(row == 0, 1.0, 0.0).astype(BF16)
    place = seq * toks + lax.broadcasted_iota(jnp.int32, (1, toks), 1)
    start = run_starts(seg_ref, bounds_ref)
    first_start = start_at(seq * toks, bounds_ref)
    peak_ref[...] = jnp.full(peak_ref.shape, NEG, F32)
    total_ref[...] = jnp.zeros(total_ref.shape, F32)
    sum_ref[...] = jnp.zeros(sum_ref.shape, F32)
    for b in range(blocks):
        block = block_of(b, seq)

        @pl.when((block >= 0) & (block <= seq) & (block * toks + toks > first_start))
        def _(b=b, block=block):
            count = k_refs[b].shape[1]
            k_aug[:att, :] = k_refs[b][...]
            pads = pay_ref[block, inner:, :].astype(F32)
            pads = jnp.concatenate([pads[i : i + 1, :] for i in range(count // 128)], axis=1)
            bias = (pads - 1.0) * 1e30
            k_aug[att:, :] = jnp.where(row == 0, bias, 0.0).astype(BF16)
            scores = (
                lax.dot_general(
                    k_aug[...], q_aug[...], (((0,), (0,)), ((), ())), preferred_element_type=F32
                )
                * score_scale
            )
            key = block * count + lax.broadcasted_iota(jnp.int32, (count, toks), 0)
            scores = jnp.where((key <= place) & (key >= start), scores, NEG)
            peak = jnp.maximum(peak_ref[...], jnp.max(scores, axis=0, keepdims=True))
            weights = jnp.exp(scores - peak)
            keep = jnp.exp(peak_ref[...] - peak)
            peak_ref[...] = peak
            total_ref[...] = total_ref[...] * keep + jnp.sum(weights, axis=0, keepdims=True)
            sum_ref[...] = sum_ref[...] * keep + jnp.dot(
                v_refs[b][...], weights.astype(BF16), preferred_element_type=F32
            )

    ctx_ref[...] = (sum_ref[...] / total_ref[...]).astype(BF16)


def last_kernel(pieces, rows, *refs):
    slots_ref = refs[0]
    piece_refs = refs[1 : 1 + pieces]
    w_ref, mixed_ref, out_ref, full_ref = refs[1 + pieces :]
    lay_out(slots_ref, piece_refs, rows, full_ref)
    product = jnp.dot(w_ref[...], full_ref[...], preferred_element_type=F32)
    out_ref[...] = (mixed_ref[...].astype(F32) + product).T.astype(BF16)


def on_device(
    tp_count,
    seq_count,
    hidden_in,
    mamba_gain,
    w_xz,
    w_bc,
    w_dt,
    dt_bias,
    decay_rate,
    conv_x,
    conv_bc,
    skip_gain,
    inner_gain,
    w_out,
    attn_gain,
    w_qkv,
    w_o,
    seg_ids,
    pad_mask,
    tenant_bounds,
):
    toks, part = hidden_in.shape
    width = mamba_gain.shape[0]
    inner = w_xz.shape[1]
    heads = decay_rate.shape[0]
    att = w_qkv.shape[1]
    tenants = tenant_bounds.shape[0]
    bc = w_bc.shape[1]
    conv_rows = inner + bc
    seq = lax.axis_index("seq")
    sds = jax.ShapeDtypeStruct

    hidden_t = hidden_in.T
    slots = jnp.asarray(sources(tp_count))
    seg_row, pad_row = seg_ids[None, :], pad_mask[None, :]

    out_share, o_share = inner // seq_count, att // seq_count

    def shares(first):
        out_rows, o_rows, _ = after((w_out, w_o), first)
        if out_share % 8 or o_share % 8:
            scaled = (out_rows.astype(F32) * inner_gain[:, None]).astype(BF16)
            cut = [
                lax.dynamic_slice_in_dim(rows, seq * count, count)
                for rows, count in ((scaled, out_share), (o_rows, o_share))
            ]
            return tuple(c.reshape(c.shape[0], tp_count, part).transpose(1, 0, 2) for c in cut)
        return pl.pallas_call(
            share_kernel,
            out_shape=(
                sds((tp_count, out_share, part), BF16),
                sds((tp_count, o_share, part), BF16),
            ),
            grid_spec=pltpu.PrefetchScalarGridSpec(
                num_scalar_prefetch=1,
                grid=(1,),
                in_specs=[
                    pl.BlockSpec((out_share, width), lambda i, at: (at[0], 0)),
                    pl.BlockSpec((o_share, width), lambda i, at: (at[0], 0)),
                    pl.BlockSpec((out_share, 128), lambda i, at: (at[0], 0)),
                ],
                out_specs=(
                    pl.BlockSpec((tp_count, out_share, part), lambda i, at: (0, 0, 0)),
                    pl.BlockSpec((tp_count, o_share, part), lambda i, at: (0, 0, 0)),
                ),
            ),
            compiler_params=pltpu.CompilerParams(vmem_limit_bytes=16 << 20),
        )(
            jnp.full((1,), seq, jnp.int32),
            out_rows,
            o_rows,
            jnp.broadcast_to(inner_gain[:, None], (inner, 128)),
        )

    in_rows = conv_rows + inner + 16

    def in_weights(first):
        xz, narrow, dt, _ = after((w_xz, w_bc, w_dt), first)
        return call(
            weights_kernel,
            sds((in_rows, width), BF16),
            (xz, narrow, dt, mamba_gain[None, :]),
            vmem=16,
            flops=10**7,
        )

    def exchange(share, first):
        value, _ = after((share,), first)
        return lax.all_to_all(value, "tp", 0, 0, tiled=False)

    def spread(columns, first):
        value, _ = after((columns,), first)
        return lax.all_gather(value, "seq", axis=1, tiled=True)

    full_in, ((out_shares, o_shares), w_in) = ring_gather(
        hidden_t, "tp", tp_count, True, ((1, 3, shares), (3, 5, in_weights))
    )
    pieces = len(full_in)

    raw, z, dt_raw, tail = call(
        functools.partial(in_kernel, pieces, part, conv_rows, inner),
        (
            sds((conv_rows, toks), F32),
            sds((inner, toks), F32),
            sds((8, toks), F32),
            sds((8, conv_rows), F32),
        ),
        (slots, *full_in, w_in),
        smem=(0,),
        scratch=[
            pltpu.VMEM((width, toks), BF16),
            pltpu.VMEM((in_rows, toks), F32),
        ],
        flops=2 * in_rows * width * toks,
    )
    w_out_cols = spread(exchange(out_shares, tail), tail)
    halo = lax.ppermute(tail, "seq", [(i, i + 1) for i in range(seq_count - 1)])
    y, c_rows, entry, pay, local = call(
        functools.partial(mix_kernel, tenants, heads),
        (
            sds((inner, toks), F32),
            sds((bc // 2, toks), BF16),
            sds((8, toks), F32),
            sds((inner + 16, 128), BF16),
            sds((tenants * inner, 128), F32),
        ),
        (tenant_bounds, dt_bias, decay_rate, skip_gain, raw, dt_raw, halo, conv_x, conv_bc, seg_row, pad_row),
        smem=(0, 1, 2, 3),
        scratch=[
            pltpu.VMEM((conv_rows, toks + 128), F32),
            pltpu.VMEM((conv_rows, toks), F32),
            pltpu.VMEM((inner, toks), F32),
            pltpu.VMEM((conv_rows, 128), F32),
        ],
        flops=10**9,
    )
    all_pays = lax.all_gather(pay, "seq", axis=0, tiled=False)
    gated, tenant_part = call(
        functools.partial(gate_kernel, tenants, heads),
        (sds((inner, toks), BF16), sds((tenants * inner, bc // 2), BF16)),
        (tenant_bounds, all_pays, y, z, c_rows, entry, local),
        smem=(0,),
        flops=10**8,
    )
    tenant_states = (
        sum_pairs(tenant_part, "seq", seq_count)
        .astype(F32)
        .reshape(tenants, heads, inner // heads, bc // 2)
    )
    def turned(cols, rows):
        def task(first):
            value, _ = after((cols,), first)
            return call(
                turn_kernel,
                sds((part, tp_count * rows), BF16),
                (value.reshape(tp_count * rows, part),),
            )

        return task

    full_gated, (w_out_t,) = ring_gather(
        gated, "tp", tp_count, False, ((3, -1, turned(w_out_cols, inner)),)
    )
    mixed = call(
        functools.partial(mixed_kernel, len(full_gated), inner),
        sds((part, toks), BF16),
        (slots, *full_gated, w_out_t, hidden_t),
        smem=(0,),
        scratch=[
            pltpu.VMEM((tp_count * inner, toks), BF16),
        ],
        flops=2 * part * tp_count * inner * toks,
    )
    def att_weights(first):
        value, _ = after((w_qkv,), first)
        return (value.reshape(3 * att, width).astype(F32) * attn_gain).astype(BF16)

    full_mixed, (w_att,) = ring_gather(mixed, "tp", tp_count, True, ((4, 5, att_weights),))
    queries, keys, values, kv = call(
        functools.partial(qkv_kernel, len(full_mixed), part),
        (
            sds((att, toks), BF16),
            sds((att, toks), BF16),
            sds((att, toks), BF16),
            sds((2 * att, toks), BF16),
        ),
        (slots, *full_mixed, w_att),
        smem=(0,),
        scratch=[
            pltpu.VMEM((width, toks), BF16),
        ],
        flops=6 * att * width * toks,
    )
    kv_cache = kv.reshape(2, att, toks)

    if seq_count == 4:

        def near(value):
            return lax.ppermute(value, "seq", [(0, 1), (2, 3)])

        def far(value):
            return lax.ppermute(value, "seq", [(0, 2), (1, 3)])

        def swap(value):
            return lax.ppermute(value, "seq", [(2, 3), (3, 2)])

        far_keys, far_values = far(keys), far(values)
        near_keys, near_values = near(keys), near(values)
        o_columns = exchange(o_shares, (near_keys, near_values))
        swap_keys, swap_values = swap(far_keys), swap(far_values)
        w_o_cols = spread(o_columns, (swap_keys, swap_values))
        key_blocks = [keys, near_keys, far_keys, swap_keys]
        value_blocks = [values, near_values, far_values, swap_values]


        def block_of(b, at):
            return (at, at ^ 1, at - 2, (at ^ 1) - 2)[b]

    else:
        all_keys = lax.all_gather(keys, "seq", axis=0, tiled=False)
        all_values = lax.all_gather(values, "seq", axis=0, tiled=False)
        w_o_cols = spread(exchange(o_shares, keys), keys)
        key_blocks = [all_keys[i] for i in range(seq_count)]
        value_blocks = [all_values[i] for i in range(seq_count)]

        def block_of(b, at):
            return jnp.int32(b)

    blocks = len(key_blocks)
    deep = att + 32
    context = call(
        functools.partial(attend_kernel, blocks, block_of, att ** (-0.5)),
        sds((att, toks), BF16),
        (tenant_bounds, queries, *key_blocks, *value_blocks, all_pays, seg_row),
        smem=(0,),
        scratch=[
            pltpu.VMEM((deep, toks), BF16),
            pltpu.VMEM((deep, toks), BF16),
            pltpu.VMEM((1, toks), F32),
            pltpu.VMEM((1, toks), F32),
            pltpu.VMEM((att, toks), F32),
        ],
        flops=4 * blocks * toks * toks * att,
    )
    full_context, (w_o_t,) = ring_gather(
        context, "tp", tp_count, False, ((1, 2, turned(w_o_cols, att)),)
    )
    hidden_out = call(
        functools.partial(last_kernel, len(full_context), att),
        sds((toks, part), BF16),
        (slots, *full_context, w_o_t, mixed),
        smem=(0,),
        scratch=[
            pltpu.VMEM((tp_count * att, toks), BF16),
        ],
        flops=2 * part * tp_count * att * toks,
    )
    return (hidden_out, kv_cache, tenant_states)


def solution(mesh):
    return jax.shard_map(
        functools.partial(on_device, mesh.shape["tp"], mesh.shape["seq"]),
        mesh=mesh,
        in_specs=(
            P("seq", "tp"),
            P(),
            P(None, "tp", None),
            P(),
            P("tp", None),
            P("tp"),
            P("tp"),
            P(None, "tp"),
            P(),
            P("tp"),
            P("tp"),
            P("tp", None),
            P(),
            P(None, "tp", None),
            P("tp", None),
            P("seq"),
            P("seq"),
            P(),
        ),
        out_specs=(P("seq", "tp"), P(None, "tp", "seq"), P(None, "tp", None, None)),
        check_vma=False,
    )
```

```python
import functools

import jax
import jax.numpy as jnp
import numpy as np
from jax import lax
from jax.experimental import pallas as pl
from jax.experimental.pallas import tpu as pltpu
from jax.sharding import PartitionSpec as P

F32 = jnp.float32
BF16 = jnp.bfloat16
EPS = 1e-05
NEG = -1e30


def ring_order(count):
    columns = {8: 2, 32: 4}.get(count, 0)
    if not columns:
        return list(range(count))
    rows = count // columns
    order = [row * columns for row in range(rows)]
    for row in reversed(range(rows)):
        inner = list(range(1, columns))
        if (rows - 1 - row) % 2:
            inner.reverse()
        order += [row * columns + column for column in inner]
    return order


def sources(count):
    order = ring_order(count)
    place = {device: i for i, device in enumerate(order)}
    table = np.zeros((count, count), np.int32)
    for device in range(count):
        at = place[device]
        slots = [order[at]]
        for hop in range(1, (count - 1) // 2 + 1):
            slots += [order[(at - hop) % count], order[(at + hop) % count]]
        if count % 2 == 0 and count > 1:
            slots.append(order[(at + count // 2) % count])
        table[device] = slots
    return table


def ring_gather(parts, axis, count, tasks=()):
    order = ring_order(count)
    ahead = [(order[i], order[(i + 1) % count]) for i in range(count)]
    behind = [(order[i], order[(i - 1) % count]) for i in range(count)]
    half = parts[0].shape[0] // 2
    split = len(parts) > 1
    far_hop = (count - 1) // 2 + 1
    last_hop = far_hop if count % 2 == 0 else far_hop - 1
    here = {(0, i): (part, part) for i, part in enumerate(parts)}
    results = [None] * len(tasks)
    finished = [tuple(parts)]
    step = 0
    for hop in range(1, last_hop + 1):
        for i in range(len(parts)):
            one, two = here[hop - 1, i]
            wait = finished[max(0, len(finished) - 3)] if split else finished[-1]
            ends = [t for t, task in enumerate(tasks) if task[1] == step - 1]
            held = [results[t] for t in ends]
            one, two, _, held = lax.optimization_barrier((one, two, wait, held))
            for t, value in zip(ends, held, strict=True):
                results[t] = value
            if hop < far_hop:
                got = (lax.ppermute(one, axis, ahead), lax.ppermute(two, axis, behind))
            elif not split and half % 16 == 0:
                got = (lax.ppermute(one[:half], axis, ahead), lax.ppermute(two[half:], axis, behind))
            elif i == 0:
                got = (lax.ppermute(one, axis, ahead),) * 2
            else:
                got = (lax.ppermute(two, axis, behind),) * 2
            here[hop, i] = got
            for t, task in enumerate(tasks):
                if task[0] == step:
                    recent = finished[max(0, step + 1 - len(parts)) :]
                    results[t] = task[2]([value for pair in recent for value in pair])
            finished.append(got)
            step += 1
    pieces = [[part] for part in parts]
    for hop in range(1, last_hop + 1):
        for i in range(len(parts)):
            if hop < far_hop or (not split and half % 16 == 0):
                pieces[i] += list(here[hop, i])
            else:
                pieces[i].append(here[hop, i][0])
    return pieces, results


def sum_pairs(value, axis, count):
    by = 1
    while by < count:
        value = value + lax.ppermute(value, axis, [(i, i ^ by) for i in range(count)])
        by *= 2
    return value


def lay_out(slots_ref, piece_refs, rows, full_ref):
    columns = full_ref.shape[1]
    total = jnp.zeros((8, columns), F32)
    slot = 0
    done = 0
    for piece in piece_refs:
        count = piece.shape[0]
        strip = next(s for s in (64, 32, 16, 8) if count % s == 0)
        start = slots_ref[lax.axis_index("tp"), slot] * rows + done

        def body(i, carry, piece=piece, strip=strip, start=start):
            part = piece[pl.ds(pl.multiple_of(i * strip, strip), strip), :]
            full_ref[pl.ds(pl.multiple_of(start + i * strip, 16), strip), :] = part
            wide = part.astype(F32)
            return carry + jnp.sum((wide * wide).reshape(strip // 8, 8, columns), axis=0)

        total = lax.fori_loop(0, count // strip, body, total)
        done += count
        if done == rows:
            slot, done = slot + 1, 0
    return jnp.sum(total, axis=0, keepdims=True)


def call(kernel, out_shape, operands, smem=(), scratch=(), flops=0, vmem=12):
    specs = [
        jax.tree.map(
            lambda _, i=i: pl.BlockSpec(memory_space=pltpu.SMEM if i in smem else pltpu.VMEM), o
        )
        for i, o in enumerate(operands)
    ]
    size = sum(o.size * o.dtype.itemsize for o in jax.tree.leaves(operands))
    return pl.pallas_call(
        kernel,
        out_shape=out_shape,
        in_specs=specs,
        out_specs=jax.tree.map(lambda _: pl.BlockSpec(memory_space=pltpu.VMEM), out_shape),
        scratch_shapes=list(scratch),
        compiler_params=pltpu.CompilerParams(vmem_limit_bytes=vmem << 20),
        cost_estimate=pl.CostEstimate(flops=flops, bytes_accessed=size, transcendentals=0),
    )(*operands)


def after(values, first):
    return lax.optimization_barrier((*values, first))


def silu(value):
    return value / (1.0 + jnp.exp(-value))


def share_kernel(seq_ref, out_ref, o_ref, gain_ref, mine_ref, mine_o_ref):
    count, part = mine_ref.shape[0], mine_ref.shape[2]
    for d in range(count):
        columns = slice(d * part, (d + 1) * part)
        scaled = out_ref[:, columns].astype(F32) * gain_ref[:, 0:1]
        mine_ref[d, :, :] = scaled.astype(BF16)
        mine_o_ref[d, :, :] = o_ref[:, columns]


def weights_kernel(xz_ref, bc_ref, dt_ref, gain_ref, w_ref):
    inner = xz_ref.shape[1]
    bc = bc_ref.shape[1]
    width = gain_ref.shape[1]
    tile = 512
    for i in range(width // tile):
        at = slice(i * tile, (i + 1) * tile)
        gain = gain_ref[:, at]

        def put(first, value, at=at, gain=gain):
            w_ref[first : first + value.shape[0], at] = (value.astype(F32) * gain).astype(BF16)

        put(0, xz_ref[0, :, at])
        put(inner, bc_ref[at, :].astype(F32).T)
        put(inner + bc, xz_ref[1, :, at])
        heads = dt_ref.shape[0]
        last = jnp.concatenate(
            [dt_ref[:, at].astype(F32), jnp.zeros((16 - heads, tile), F32)], axis=0
        )
        put(2 * inner + bc, last)


def run_starts(seg_ref, bounds_ref):
    seg = seg_ref[...]
    start = jnp.zeros(seg.shape, jnp.int32)
    for t in range(bounds_ref.shape[0]):
        start = jnp.where(seg == t, bounds_ref[t, 0], start)
    return start


def start_at(place, bounds_ref):
    start = jnp.int32(0)
    for t in range(bounds_ref.shape[0]):
        start = jnp.where(place >= bounds_ref[t, 0], bounds_ref[t, 0], start)
    return start


def turn_kernel(cols_ref, out_ref):
    rows = cols_ref.shape[0]
    tile = 256 if rows % 256 == 0 else rows
    for i in range(rows // tile):
        at = slice(i * tile, (i + 1) * tile)
        out_ref[:, at] = cols_ref[at, :].astype(F32).T.astype(BF16)


def in_kernel(pieces, rows, conv_rows, inner, *refs):
    slots_ref = refs[0]
    piece_refs = refs[1 : 1 + pieces]
    w_ref, raw_ref, z_ref, dt_ref, tail_ref, full_ref, acc_ref = refs[1 + pieces :]
    squares = lay_out(slots_ref, piece_refs, rows, full_ref)
    scale = lax.rsqrt(squares / full_ref.shape[0] + EPS)
    acc_ref[...] = jnp.dot(w_ref[...], full_ref[...], preferred_element_type=F32)
    raw_ref[...] = acc_ref[:conv_rows, :] * scale
    z_ref[...] = acc_ref[conv_rows : conv_rows + inner, :] * scale
    dt_ref[...] = acc_ref[conv_rows + inner : conv_rows + inner + 8, :] * scale
    last = raw_ref.shape[1] - 128
    tail_ref[...] = raw_ref[:, last:].T[120:, :]


def mix_kernel(
    tenants,
    heads,
    bounds_ref,
    bias_ref,
    rate_ref,
    skip_ref,
    raw_refs,
    dt_refs,
    halo_ref,
    conv_x_ref,
    conv_bc_ref,
    seg_ref,
    live_ref,
    y_ref,
    c_ref,
    entry_ref,
    pay_ref,
    local_ref,
    ext_ref,
    x_ref,
    xdt_ref,
    taps_ref,
):
    conv_rows, half = raw_refs[0].shape
    toks = half * len(raw_refs)
    inner = y_ref.shape[0]
    hd = inner // heads
    lane = lax.broadcasted_iota(jnp.int32, (1, toks), 1)
    base = lax.axis_index("seq") * toks
    rel = base + lane - run_starts(seg_ref, bounds_ref)
    live = live_ref[...].astype(F32)
    count = conv_x_ref.shape[0]
    both = jnp.concatenate([conv_x_ref[...], conv_bc_ref[...]], axis=1)
    taps_ref[...] = jnp.concatenate([both, jnp.zeros((128 - count, conv_rows), F32)], axis=0).T
    head = lax.broadcasted_iota(jnp.int32, (8, 1), 0)
    bias = rate = jnp.zeros((8, 1), F32)
    for h in range(heads):
        bias = jnp.where(head == h, bias_ref[h], bias)
        rate = jnp.where(head == h, rate_ref[h], rate)
    before = jnp.concatenate([jnp.zeros((120, conv_rows), F32), halo_ref[...]], axis=0).T
    ext_ref[:, :128] = before
    for i, raw_ref in enumerate(raw_refs):
        ext_ref[:, 128 + i * half : 128 + (i + 1) * half] = raw_ref[...]
    strip = 64
    keep = [(rel >= shift).astype(F32) for shift in range(4)]
    for i in range(conv_rows // strip):
        rows = pl.ds(i * strip, strip)
        ext = ext_ref[rows, :]
        taps = taps_ref[rows, :]
        total = taps[:, 3:4] * ext[:, 128:]
        for shift in range(1, 4):
            moved = pltpu.roll(ext, shift, 1)[:, 128:]
            total = total + taps[:, 3 - shift : 4 - shift] * moved * keep[shift]
        x_ref[rows, :] = silu(total)
    step = jnp.concatenate([dt_ref[...] for dt_ref in dt_refs], axis=1) + bias
    step = (jnp.maximum(step, 0.0) + jnp.log1p(jnp.exp(-jnp.abs(step)))) * live
    logs = -step * rate
    shift = 1
    while shift < toks:
        logs = logs + jnp.where(lane >= shift, pltpu.roll(logs, shift, 1), 0.0)
        shift *= 2
    start = lane - rel
    entry_ref[...] = jnp.exp(logs) * (start < 0).astype(F32)
    for h in range(heads):
        xdt_ref[h * hd : (h + 1) * hd, :] = x_ref[h * hd : (h + 1) * hd, :] * step[h : h + 1, :]
    input_b = x_ref[inner : inner + 64, :]
    output_c = x_ref[inner + 64 : inner + 128, :].astype(BF16)
    c_ref[...] = output_c
    bc_tok = x_ref[inner : inner + 128, :].T
    b_tok = bc_tok[:, :64].astype(BF16)
    columns = [
        jnp.broadcast_to(logs[h : h + 1, :], (128, toks)).T for h in range(heads)
    ]
    for block in range(toks // 128):
        here = slice(block * 128, (block + 1) * 128)
        upto = (block + 1) * 128
        key = lax.broadcasted_iota(jnp.int32, (upto, 128), 0)
        seen = (key <= lane[:, here]) & (key >= start[:, here])
        bias = jnp.where(seen, 0.0, NEG)
        c_dot_b = jnp.dot(b_tok[:upto, :], output_c[:, here], preferred_element_type=F32)
        for h in range(heads):
            gap = logs[h : h + 1, here] - columns[h][:upto, :]
            mixing = (jnp.exp(jnp.minimum(gap, 0.0) + bias) * c_dot_b).astype(BF16)
            rows = slice(h * hd, (h + 1) * hd)
            y_ref[rows, here] = (
                jnp.dot(
                    xdt_ref[rows, :upto].astype(BF16), mixing, preferred_element_type=F32
                )
                + skip_ref[h] * x_ref[rows, here]
            )
    wide_b = bc_tok.astype(BF16)
    tok = lax.broadcasted_iota(jnp.int32, (inner, 128), 1)
    for k in range(tenants + 1):
        if k < tenants:
            pick = jnp.clip(bounds_ref[k, 1] - 1 - base, 0, toks - 1)
            first = bounds_ref[k, 0] - base
        else:
            pick = toks - 1
            first = start_at(base + toks - 1, bounds_ref) - base
        at = jnp.sum(jnp.where(lane == pick, logs, 0.0), axis=1, keepdims=True)
        inside = (lane <= pick) & (lane >= first)
        toward = jnp.exp(jnp.minimum(at - logs, 0.0) + jnp.where(inside, 0.0, NEG))
        carried = jnp.exp(at) * jnp.where(first < 0, 1.0, 0.0)
        lhs = jnp.concatenate(
            [
                (xdt_ref[h * hd : (h + 1) * hd, :] * toward[h : h + 1, :]).astype(BF16)
                for h in range(heads)
            ],
            axis=0,
        )
        state = jnp.dot(lhs, wide_b, preferred_element_type=F32)
        factor = jnp.concatenate(
            [jnp.broadcast_to(carried[h : h + 1, :], (hd, 128)) for h in range(heads)], axis=0
        )
        if k < tenants:
            local_ref[k * inner : (k + 1) * inner, :] = jnp.where(tok < 64, state, factor)
        else:
            high = factor.astype(BF16).astype(F32)
            packed = jnp.where(tok < 64, state, jnp.where(tok < 96, high, factor - high))
            pay_ref[:inner, :] = packed.astype(BF16)
    rows = [live[:, i * 128 : (i + 1) * 128] for i in range(toks // 128)]
    rows.append(jnp.zeros((16 - toks // 128, 128), F32))
    pay_ref[inner:, :] = jnp.concatenate(rows, axis=0).astype(BF16)


def gate_kernel(
    tenants,
    heads,
    bounds_ref,
    pay_ref,
    y_ref,
    z_refs,
    c_ref,
    entry_ref,
    local_ref,
    g_ref,
    tenant_ref,
):
    inner = y_ref.shape[0]
    half = z_refs[0].shape[1]
    hd = inner // heads
    incoming = jnp.zeros((inner, 64), F32)
    for block in range(pay_ref.shape[0] - 1):
        wide = pay_ref[block, :inner, :].astype(F32)
        passed = (wide[:, 64:65] + wide[:, 96:97]) * incoming + wide[:, :64]
        incoming = jnp.where(block < lax.axis_index("seq"), passed, incoming)
    for h in range(heads):
        rows = slice(h * hd, (h + 1) * hd)
        carry = jnp.dot(incoming[rows, :].astype(BF16), c_ref[...], preferred_element_type=F32)
        y_full = y_ref[rows, :] + carry * entry_ref[h : h + 1, :]
        for i, z_ref in enumerate(z_refs):
            here = slice(i * half, (i + 1) * half)
            g_ref[rows, here] = (y_full[:, here] * silu(z_ref[rows, :])).astype(BF16)
    for k in range(tenants):
        rows = slice(k * inner, (k + 1) * inner)
        last = bounds_ref[k, 1] - 1 - lax.axis_index("seq") * y_ref.shape[1]
        owned = jnp.where((last >= 0) & (last < y_ref.shape[1]), 1.0, 0.0)
        local = local_ref[rows, :]
        tenant_ref[rows, :] = ((local[:, 64:65] * incoming + local[:, :64]) * owned).astype(BF16)


def mixed_kernel(pieces, rows, *refs):
    slots_ref = refs[0]
    piece_refs = refs[1 : 1 + pieces]
    w_ref, hidden_refs, *out_refs, full_ref = refs[1 + pieces :]
    squares = lay_out(slots_ref, piece_refs, rows, full_ref)
    scale = lax.rsqrt(squares / full_ref.shape[0] + EPS)
    product = jnp.dot(w_ref[...], full_ref[...], preferred_element_type=F32) * scale
    half = out_refs[0].shape[1]
    for i, (hidden_ref, out_ref) in enumerate(zip(hidden_refs, out_refs, strict=True)):
        here = slice(i * half, (i + 1) * half)
        out_ref[...] = (hidden_ref[...].astype(F32) + product[:, here]).astype(BF16)


def qkv_kernel(rows, slots_ref, piece_refs, w_ref, first_refs, q_ref, kv_ref, all_refs, full_ref):
    squares = lay_out(slots_ref, piece_refs, rows, full_ref)
    scale = lax.rsqrt(squares / full_ref.shape[0] + EPS)
    product = jnp.dot(w_ref[...], full_ref[...], preferred_element_type=F32)
    att, half = q_ref.shape
    q_ref[...] = (product[:att] * scale).astype(BF16)
    kv_ref[...] = (product[att:] * scale).astype(BF16)
    for first_ref, all_ref in zip(first_refs, all_refs, strict=True):
        all_ref[:, :half] = first_ref[...]
        all_ref[:, half:] = kv_ref[...]


def attend_kernel(blocks, block_of, score_scale, *refs):
    bounds_ref, q_refs, kv_refs, pay_ref, seg_ref = refs[:5]
    ctx_ref, q_aug, k_aug, v_all, peak_ref, total_ref, sum_ref = refs[5:]
    inner = pay_ref.shape[1] - 16
    seq = lax.axis_index("seq")
    att, toks = ctx_ref.shape
    half = q_refs[0].shape[1]
    extra = q_aug.shape[0] - att
    row = lax.broadcasted_iota(jnp.int32, (extra, toks), 0)
    for i, q_ref in enumerate(q_refs):
        q_aug[:att, i * half : (i + 1) * half] = q_ref[...]
    q_aug[att:, :] = jnp.where(row == 0, 1.0, 0.0).astype(BF16)
    place = seq * toks + lax.broadcasted_iota(jnp.int32, (1, toks), 1)
    start = run_starts(seg_ref, bounds_ref)
    first_start = start_at(seq * toks, bounds_ref)
    peak_ref[...] = jnp.full(peak_ref.shape, NEG, F32)
    total_ref[...] = jnp.zeros(total_ref.shape, F32)
    sum_ref[...] = jnp.zeros(sum_ref.shape, F32)
    for b in range(blocks):
        block = block_of(b, seq)

        @pl.when((block >= 0) & (block <= seq) & (block * toks + toks > first_start))
        def _(b=b, block=block):
            count = toks
            for i, kv_ref in enumerate(kv_refs[b]):
                k_aug[:att, i * half : (i + 1) * half] = kv_ref[:att, :]
                v_all[:, i * half : (i + 1) * half] = kv_ref[att:, :]
            pads = pay_ref[block, inner:, :].astype(F32)
            pads = jnp.concatenate([pads[i : i + 1, :] for i in range(count // 128)], axis=1)
            bias = (pads - 1.0) * 1e30
            k_aug[att:, :] = jnp.where(row == 0, bias, 0.0).astype(BF16)
            scores = (
                lax.dot_general(
                    k_aug[...], q_aug[...], (((0,), (0,)), ((), ())), preferred_element_type=F32
                )
                * score_scale
            )
            key = block * count + lax.broadcasted_iota(jnp.int32, (count, toks), 0)
            scores = jnp.where((key <= place) & (key >= start), scores, NEG)
            peak = jnp.maximum(peak_ref[...], jnp.max(scores, axis=0, keepdims=True))
            weights = jnp.exp(scores - peak)
            keep = jnp.exp(peak_ref[...] - peak)
            peak_ref[...] = peak
            total_ref[...] = total_ref[...] * keep + jnp.sum(weights, axis=0, keepdims=True)
            sum_ref[...] = sum_ref[...] * keep + jnp.dot(
                v_all[...], weights.astype(BF16), preferred_element_type=F32
            )

    ctx_ref[...] = (sum_ref[...] / total_ref[...]).astype(BF16)


def last_kernel(pieces, rows, *refs):
    slots_ref = refs[0]
    piece_refs = refs[1 : 1 + pieces]
    w_ref, mixed_refs, out_ref, full_ref = refs[1 + pieces :]
    lay_out(slots_ref, piece_refs, rows, full_ref)
    product = jnp.dot(w_ref[...], full_ref[...], preferred_element_type=F32)
    half = mixed_refs[0].shape[1]
    for i, mixed_ref in enumerate(mixed_refs):
        here = slice(i * half, (i + 1) * half)
        out_ref[here, :] = (mixed_ref[...].astype(F32) + product[:, here]).T.astype(BF16)


def on_device(
    tp_count,
    seq_count,
    hidden_in,
    mamba_gain,
    w_xz,
    w_bc,
    w_dt,
    dt_bias,
    decay_rate,
    conv_x,
    conv_bc,
    skip_gain,
    inner_gain,
    w_out,
    attn_gain,
    w_qkv,
    w_o,
    seg_ids,
    pad_mask,
    tenant_bounds,
):
    toks, part = hidden_in.shape
    width = mamba_gain.shape[0]
    inner = w_xz.shape[1]
    heads = decay_rate.shape[0]
    att = w_qkv.shape[1]
    tenants = tenant_bounds.shape[0]
    bc = w_bc.shape[1]
    conv_rows = inner + bc
    seq = lax.axis_index("seq")
    sds = jax.ShapeDtypeStruct

    halves = 2
    half = toks // halves
    hidden_t = [hidden_in[i * half : (i + 1) * half].T for i in range(halves)]
    slots = jnp.asarray(sources(tp_count))
    seg_row, pad_row = seg_ids[None, :], pad_mask[None, :]

    out_share, o_share = inner // seq_count, att // seq_count

    def shares(first):
        out_rows, o_rows, _ = after((w_out, w_o), first)
        if out_share % 8 or o_share % 8:
            scaled = (out_rows.astype(F32) * inner_gain[:, None]).astype(BF16)
            cut = [
                lax.dynamic_slice_in_dim(rows, seq * count, count)
                for rows, count in ((scaled, out_share), (o_rows, o_share))
            ]
            return tuple(c.reshape(c.shape[0], tp_count, part).transpose(1, 0, 2) for c in cut)
        return pl.pallas_call(
            share_kernel,
            out_shape=(
                sds((tp_count, out_share, part), BF16),
                sds((tp_count, o_share, part), BF16),
            ),
            grid_spec=pltpu.PrefetchScalarGridSpec(
                num_scalar_prefetch=1,
                grid=(1,),
                in_specs=[
                    pl.BlockSpec((out_share, width), lambda i, at: (at[0], 0)),
                    pl.BlockSpec((o_share, width), lambda i, at: (at[0], 0)),
                    pl.BlockSpec((out_share, 128), lambda i, at: (at[0], 0)),
                ],
                out_specs=(
                    pl.BlockSpec((tp_count, out_share, part), lambda i, at: (0, 0, 0)),
                    pl.BlockSpec((tp_count, o_share, part), lambda i, at: (0, 0, 0)),
                ),
            ),
            compiler_params=pltpu.CompilerParams(vmem_limit_bytes=16 << 20),
        )(
            jnp.full((1,), seq, jnp.int32),
            out_rows,
            o_rows,
            jnp.broadcast_to(inner_gain[:, None], (inner, 128)),
        )

    in_rows = conv_rows + inner + 16

    def in_weights(first):
        xz, narrow, dt, _ = after((w_xz, w_bc, w_dt), first)
        return call(
            weights_kernel,
            sds((in_rows, width), BF16),
            (xz, narrow, dt, mamba_gain[None, :]),
            vmem=16,
            flops=10**7,
        )

    def exchange(share, first):
        value, _ = after((share,), first)
        return lax.all_to_all(value, "tp", 0, 0, tiled=False)

    def spread(columns, first):
        value, _ = after((columns,), first)
        return lax.all_gather(value, "seq", axis=1, tiled=True)

    full_in, ((out_shares, o_shares), w_in) = ring_gather(
        hidden_t, "tp", tp_count, ((1, 3, shares), (3, 5, in_weights))
    )
    pieces = len(full_in[0])

    raws, zs, dts, tails = zip(
        *(
            call(
                functools.partial(in_kernel, pieces, part, conv_rows, inner),
                (
                    sds((conv_rows, half), F32),
                    sds((inner, half), F32),
                    sds((8, half), F32),
                    sds((8, conv_rows), F32),
                ),
                (slots, *full, w_in),
                smem=(0,),
                scratch=[pltpu.VMEM((width, half), BF16), pltpu.VMEM((in_rows, half), F32)],
                flops=2 * in_rows * width * half,
            )
            for full in full_in
        ),
        strict=True,
    )
    tail = tails[-1]
    out_columns = exchange(out_shares, tails)
    halo = lax.ppermute(tail, "seq", [(i, i + 1) for i in range(seq_count - 1)])
    y, c_rows, entry, pay, local = call(
        functools.partial(mix_kernel, tenants, heads),
        (
            sds((inner, toks), F32),
            sds((bc // 2, toks), BF16),
            sds((8, toks), F32),
            sds((inner + 16, 128), BF16),
            sds((tenants * inner, 128), F32),
        ),
        (tenant_bounds, dt_bias, decay_rate, skip_gain, raws, dts, halo, conv_x, conv_bc, seg_row, pad_row),
        smem=(0, 1, 2, 3),
        scratch=[
            pltpu.VMEM((conv_rows, toks + 128), F32),
            pltpu.VMEM((conv_rows, toks), F32),
            pltpu.VMEM((inner, toks), F32),
            pltpu.VMEM((conv_rows, 128), F32),
        ],
        flops=10**9,
    )
    w_out_cols = spread(out_columns, pay)
    all_pays = lax.all_gather(pay, "seq", axis=0, tiled=False)
    gated, tenant_part = call(
        functools.partial(gate_kernel, tenants, heads),
        (
            sds((inner, toks), BF16),
            sds((tenants * inner, bc // 2), BF16),
        ),
        (tenant_bounds, all_pays, y, zs, c_rows, entry, local),
        smem=(0,),
        flops=10**8,
    )
    def tenant_sums(first):
        value, _ = after((tenant_part,), first)
        return sum_pairs(value, "seq", seq_count)

    def turned(cols, rows):
        def task(first):
            value, _ = after((cols,), first)
            return call(
                turn_kernel,
                sds((part, tp_count * rows), BF16),
                (value.reshape(tp_count * rows, part),),
            )

        return task

    (full_gated,), (tenant_sum, w_out_t) = ring_gather(
        [gated], "tp", tp_count, ((0, 2, tenant_sums), (3, -1, turned(w_out_cols, inner)))
    )
    tenant_states = tenant_sum.astype(F32).reshape(tenants, heads, inner // heads, bc // 2)
    mixed = call(
        functools.partial(mixed_kernel, len(full_gated), inner),
        [sds((part, half), BF16) for _ in range(halves)],
        (slots, *full_gated, w_out_t, hidden_t),
        smem=(0,),
        scratch=[pltpu.VMEM((tp_count * inner, toks), BF16)],
        flops=2 * part * tp_count * inner * toks,
    )

    def att_weights(first):
        value, _ = after((w_qkv,), first)
        return (value.reshape(3 * att, width).astype(F32) * attn_gain).astype(BF16)

    full_mixed, (w_att,) = ring_gather(mixed, "tp", tp_count, ((4, 5, att_weights),))
    queries, kvs = [], []
    for i, full in enumerate(full_mixed):
        last = i == halves - 1
        q_half, kv_half, whole = call(
            functools.partial(qkv_kernel, part),
            (
                sds((att, half), BF16),
                sds((2 * att, half), BF16),
                [sds((2 * att, toks), BF16)] if last else [],
            ),
            (slots, full, w_att, kvs if last else []),
            smem=(0,),
            scratch=[pltpu.VMEM((width, half), BF16)],
            flops=6 * att * width * half,
        )
        queries.append(q_half)
        kvs.append(kv_half)
    kv_cache = whole[0].reshape(2, att, toks)

    if seq_count == 4:

        def near(value):
            return lax.ppermute(value, "seq", [(0, 1), (2, 3)])

        def far(value):
            return lax.ppermute(value, "seq", [(0, 2), (1, 3)])

        def swap(value):
            return lax.ppermute(value, "seq", [(2, 3), (3, 2)])

        fars = [far(kv) for kv in kvs]
        nears = [near(kv) for kv in kvs]
        o_columns = exchange(o_shares, (fars, nears))
        swaps = [swap(kv) for kv in fars]
        w_o_cols = spread(o_columns, swaps)
        kv_blocks = [kvs, nears, fars, swaps]

        def block_of(b, at):
            return (at, at ^ 1, at - 2, (at ^ 1) - 2)[b]

    else:
        all_kv = [lax.all_gather(kv, "seq", axis=0, tiled=False) for kv in kvs]
        w_o_cols = spread(exchange(o_shares, kvs), kvs)
        kv_blocks = [[kv[i] for kv in all_kv] for i in range(seq_count)]

        def block_of(b, at):
            return jnp.int32(b)

    blocks = len(kv_blocks)
    deep = att + 32
    context = call(
        functools.partial(attend_kernel, blocks, block_of, att ** (-0.5)),
        sds((att, toks), BF16),
        (tenant_bounds, queries, kv_blocks, all_pays, seg_row),
        smem=(0,),
        scratch=[
            pltpu.VMEM((deep, toks), BF16),
            pltpu.VMEM((deep, toks), BF16),
            pltpu.VMEM((att, toks), BF16),
            pltpu.VMEM((1, toks), F32),
            pltpu.VMEM((1, toks), F32),
            pltpu.VMEM((att, toks), F32),
        ],
        flops=4 * blocks * toks * toks * att,
    )
    (full_context,), (w_o_t,) = ring_gather(
        [context], "tp", tp_count, ((1, 2, turned(w_o_cols, att)),)
    )
    hidden_out = call(
        functools.partial(last_kernel, len(full_context), att),
        sds((toks, part), BF16),
        (slots, *full_context, w_o_t, mixed),
        smem=(0,),
        scratch=[
            pltpu.VMEM((tp_count * att, toks), BF16),
        ],
        flops=2 * part * tp_count * att * toks,
    )
    return (hidden_out, kv_cache, tenant_states)


def solution(mesh):
    return jax.shard_map(
        functools.partial(on_device, mesh.shape["tp"], mesh.shape["seq"]),
        mesh=mesh,
        in_specs=(
            P("seq", "tp"),
            P(),
            P(None, "tp", None),
            P(),
            P("tp", None),
            P("tp"),
            P("tp"),
            P(None, "tp"),
            P(),
            P("tp"),
            P("tp"),
            P("tp", None),
            P(),
            P(None, "tp", None),
            P("tp", None),
            P("seq"),
            P("seq"),
            P(),
        ),
        out_specs=(P("seq", "tp"), P(None, "tp", "seq"), P(None, "tp", None, None)),
        check_vma=False,
    )
```

```python
import functools

import jax
import jax.numpy as jnp
import numpy as np
from jax import lax
from jax.experimental import pallas as pl
from jax.experimental.pallas import tpu as pltpu
from jax.sharding import PartitionSpec as P

F32 = jnp.float32
BF16 = jnp.bfloat16
EPS = 1e-05
NEG = -1e30


def ring_order(count):
    columns = {8: 2, 32: 4}.get(count, 0)
    if not columns:
        return list(range(count))
    rows = count // columns
    order = [row * columns for row in range(rows)]
    for row in reversed(range(rows)):
        inner = list(range(1, columns))
        if (rows - 1 - row) % 2:
            inner.reverse()
        order += [row * columns + column for column in inner]
    return order


def sources(count):
    order = ring_order(count)
    place = {device: i for i, device in enumerate(order)}
    table = np.zeros((count, count), np.int32)
    for device in range(count):
        at = place[device]
        slots = [order[at]]
        for hop in range(1, (count - 1) // 2 + 1):
            slots += [order[(at - hop) % count], order[(at + hop) % count]]
        if count % 2 == 0 and count > 1:
            slots.append(order[(at + count // 2) % count])
        table[device] = slots
    return table


def ring_gather(parts, axis, count, tasks=()):
    order = ring_order(count)
    ahead = [(order[i], order[(i + 1) % count]) for i in range(count)]
    behind = [(order[i], order[(i - 1) % count]) for i in range(count)]
    half = parts[0].shape[0] // 2
    split = len(parts) > 1
    far_hop = (count - 1) // 2 + 1
    last_hop = far_hop if count % 2 == 0 else far_hop - 1
    here = {(0, i): (part, part) for i, part in enumerate(parts)}
    results = [None] * len(tasks)
    finished = [tuple(parts)]
    step = 0
    for hop in range(1, last_hop + 1):
        for i in range(len(parts)):
            one, two = here[hop - 1, i]
            wait = finished[max(0, len(finished) - 3)] if split else finished[-1]
            ends = [t for t, task in enumerate(tasks) if task[1] == step - 1]
            held = [results[t] for t in ends]
            one, two, _, held = lax.optimization_barrier((one, two, wait, held))
            for t, value in zip(ends, held, strict=True):
                results[t] = value
            if hop < far_hop:
                got = (lax.ppermute(one, axis, ahead), lax.ppermute(two, axis, behind))
            elif not split and half % 16 == 0:
                got = (lax.ppermute(one[:half], axis, ahead), lax.ppermute(two[half:], axis, behind))
            elif i == 0:
                got = (lax.ppermute(one, axis, ahead),) * 2
            else:
                got = (lax.ppermute(two, axis, behind),) * 2
            here[hop, i] = got
            for t, task in enumerate(tasks):
                if task[0] == step:
                    recent = finished[max(0, step + 1 - len(parts)) :]
                    results[t] = task[2]([value for pair in recent for value in pair])
            finished.append(got)
            step += 1
    pieces = [[part] for part in parts]
    for hop in range(1, last_hop + 1):
        for i in range(len(parts)):
            if hop < far_hop or (not split and half % 16 == 0):
                pieces[i] += list(here[hop, i])
            else:
                pieces[i].append(here[hop, i][0])
    return pieces, results


def sum_pairs(value, axis, count):
    by = 1
    while by < count:
        value = value + lax.ppermute(value, axis, [(i, i ^ by) for i in range(count)])
        by *= 2
    return value


def lay_out(slots_ref, piece_refs, rows, full_ref):
    columns = full_ref.shape[1]
    total = jnp.zeros((8, columns), F32)
    slot = 0
    done = 0
    for piece in piece_refs:
        count = piece.shape[0]
        strip = next(s for s in (64, 32, 16, 8) if count % s == 0)
        start = slots_ref[lax.axis_index("tp"), slot] * rows + done

        def body(i, carry, piece=piece, strip=strip, start=start):
            part = piece[pl.ds(pl.multiple_of(i * strip, strip), strip), :]
            full_ref[pl.ds(pl.multiple_of(start + i * strip, 16), strip), :] = part
            wide = part.astype(F32)
            return carry + jnp.sum((wide * wide).reshape(strip // 8, 8, columns), axis=0)

        total = lax.fori_loop(0, count // strip, body, total)
        done += count
        if done == rows:
            slot, done = slot + 1, 0
    return jnp.sum(total, axis=0, keepdims=True)


def call(kernel, out_shape, operands, smem=(), scratch=(), flops=0, vmem=12):
    specs = [
        jax.tree.map(
            lambda _, i=i: pl.BlockSpec(memory_space=pltpu.SMEM if i in smem else pltpu.VMEM), o
        )
        for i, o in enumerate(operands)
    ]
    size = sum(o.size * o.dtype.itemsize for o in jax.tree.leaves(operands))
    return pl.pallas_call(
        kernel,
        out_shape=out_shape,
        in_specs=specs,
        out_specs=jax.tree.map(lambda _: pl.BlockSpec(memory_space=pltpu.VMEM), out_shape),
        scratch_shapes=list(scratch),
        compiler_params=pltpu.CompilerParams(vmem_limit_bytes=vmem << 20),
        cost_estimate=pl.CostEstimate(flops=flops, bytes_accessed=size, transcendentals=0),
    )(*operands)


def after(values, first):
    return lax.optimization_barrier((*values, first))


def silu(value):
    return value / (1.0 + jnp.exp(-value))


def share_kernel(seq_ref, out_ref, o_ref, gain_ref, mine_ref, mine_o_ref):
    count, part = mine_ref.shape[0], mine_ref.shape[2]
    for d in range(count):
        columns = slice(d * part, (d + 1) * part)
        scaled = out_ref[:, columns].astype(F32) * gain_ref[:, 0:1]
        mine_ref[d, :, :] = scaled.astype(BF16)
        mine_o_ref[d, :, :] = o_ref[:, columns]


def weights_kernel(xz_ref, bc_ref, dt_ref, gain_ref, w_ref):
    inner = xz_ref.shape[1]
    bc = bc_ref.shape[1]
    width = gain_ref.shape[1]
    tile = 512
    for i in range(width // tile):
        at = slice(i * tile, (i + 1) * tile)
        gain = gain_ref[:, at]

        def put(first, value, at=at, gain=gain):
            w_ref[first : first + value.shape[0], at] = (value.astype(F32) * gain).astype(BF16)

        put(0, xz_ref[0, :, at])
        put(inner, bc_ref[at, :].astype(F32).T)
        put(inner + bc, xz_ref[1, :, at])
        heads = dt_ref.shape[0]
        last = jnp.concatenate(
            [dt_ref[:, at].astype(F32), jnp.zeros((16 - heads, tile), F32)], axis=0
        )
        put(2 * inner + bc, last)


def run_starts(seg_ref, bounds_ref):
    seg = seg_ref[...]
    start = jnp.zeros(seg.shape, jnp.int32)
    for t in range(bounds_ref.shape[0]):
        start = jnp.where(seg == t, bounds_ref[t, 0], start)
    return start


def start_at(place, bounds_ref):
    start = jnp.int32(0)
    for t in range(bounds_ref.shape[0]):
        start = jnp.where(place >= bounds_ref[t, 0], bounds_ref[t, 0], start)
    return start


def turn_kernel(cols_ref, out_ref):
    rows = cols_ref.shape[0]
    tile = 256 if rows % 256 == 0 else rows
    for i in range(rows // tile):
        at = slice(i * tile, (i + 1) * tile)
        out_ref[:, at] = cols_ref[at, :].astype(F32).T.astype(BF16)


def in_kernel(pieces, rows, conv_rows, inner, *refs):
    slots_ref = refs[0]
    piece_refs = refs[1 : 1 + pieces]
    w_ref, raw_ref, z_ref, dt_ref, tail_ref, full_ref, acc_ref = refs[1 + pieces :]
    squares = lay_out(slots_ref, piece_refs, rows, full_ref)
    scale = lax.rsqrt(squares / full_ref.shape[0] + EPS)
    acc_ref[...] = jnp.dot(w_ref[...], full_ref[...], preferred_element_type=F32)
    raw_ref[...] = acc_ref[:conv_rows, :] * scale
    z_ref[...] = acc_ref[conv_rows : conv_rows + inner, :] * scale
    dt_ref[...] = acc_ref[conv_rows + inner : conv_rows + inner + 8, :] * scale
    last = raw_ref.shape[1] - 128
    tail_ref[...] = raw_ref[:, last:].T[120:, :]


def mix_kernel(
    tenants,
    heads,
    bounds_ref,
    bias_ref,
    rate_ref,
    skip_ref,
    raw_refs,
    dt_refs,
    halo_ref,
    conv_x_ref,
    conv_bc_ref,
    seg_ref,
    live_ref,
    y_ref,
    c_ref,
    entry_ref,
    pay_ref,
    local_ref,
    ext_ref,
    x_ref,
    xdt_ref,
    taps_ref,
):
    conv_rows, half = raw_refs[0].shape
    toks = half * len(raw_refs)
    inner = y_ref.shape[0]
    hd = inner // heads
    lane = lax.broadcasted_iota(jnp.int32, (1, toks), 1)
    base = lax.axis_index("seq") * toks
    rel = base + lane - run_starts(seg_ref, bounds_ref)
    live = live_ref[...].astype(F32)
    count = conv_x_ref.shape[0]
    both = jnp.concatenate([conv_x_ref[...], conv_bc_ref[...]], axis=1)
    taps_ref[...] = jnp.concatenate([both, jnp.zeros((128 - count, conv_rows), F32)], axis=0).T
    head = lax.broadcasted_iota(jnp.int32, (8, 1), 0)
    bias = rate = jnp.zeros((8, 1), F32)
    for h in range(heads):
        bias = jnp.where(head == h, bias_ref[h], bias)
        rate = jnp.where(head == h, rate_ref[h], rate)
    before = jnp.concatenate([jnp.zeros((120, conv_rows), F32), halo_ref[...]], axis=0).T
    ext_ref[:, :128] = before
    for i, raw_ref in enumerate(raw_refs):
        ext_ref[:, 128 + i * half : 128 + (i + 1) * half] = raw_ref[...]
    strip = 64
    keep = [(rel >= shift).astype(F32) for shift in range(4)]
    for i in range(conv_rows // strip):
        rows = pl.ds(i * strip, strip)
        ext = ext_ref[rows, :]
        taps = taps_ref[rows, :]
        total = taps[:, 3:4] * ext[:, 128:]
        for shift in range(1, 4):
            moved = pltpu.roll(ext, shift, 1)[:, 128:]
            total = total + taps[:, 3 - shift : 4 - shift] * moved * keep[shift]
        x_ref[rows, :] = silu(total)
    step = jnp.concatenate([dt_ref[...] for dt_ref in dt_refs], axis=1) + bias
    step = (jnp.maximum(step, 0.0) + jnp.log1p(jnp.exp(-jnp.abs(step)))) * live
    logs = -step * rate
    shift = 1
    while shift < toks:
        logs = logs + jnp.where(lane >= shift, pltpu.roll(logs, shift, 1), 0.0)
        shift *= 2
    start = lane - rel
    entry_ref[...] = jnp.exp(logs) * (start < 0).astype(F32)
    for h in range(heads):
        xdt_ref[h * hd : (h + 1) * hd, :] = x_ref[h * hd : (h + 1) * hd, :] * step[h : h + 1, :]
    input_b = x_ref[inner : inner + 64, :]
    output_c = x_ref[inner + 64 : inner + 128, :].astype(BF16)
    c_ref[...] = output_c
    bc_tok = x_ref[inner : inner + 128, :].T
    b_tok = bc_tok[:, :64].astype(BF16)
    columns = [
        jnp.broadcast_to(logs[h : h + 1, :], (128, toks)).T for h in range(heads)
    ]
    for block in range(toks // 128):
        here = slice(block * 128, (block + 1) * 128)
        upto = (block + 1) * 128
        key = lax.broadcasted_iota(jnp.int32, (upto, 128), 0)
        seen = (key <= lane[:, here]) & (key >= start[:, here])
        bias = jnp.where(seen, 0.0, NEG)
        c_dot_b = jnp.dot(b_tok[:upto, :], output_c[:, here], preferred_element_type=F32)
        for h in range(heads):
            gap = logs[h : h + 1, here] - columns[h][:upto, :]
            mixing = (jnp.exp(jnp.minimum(gap, 0.0) + bias) * c_dot_b).astype(BF16)
            rows = slice(h * hd, (h + 1) * hd)
            y_ref[rows, here] = (
                jnp.dot(
                    xdt_ref[rows, :upto].astype(BF16), mixing, preferred_element_type=F32
                )
                + skip_ref[h] * x_ref[rows, here]
            )
    wide_b = bc_tok.astype(BF16)
    tok = lax.broadcasted_iota(jnp.int32, (inner, 128), 1)
    for k in range(tenants + 1):
        if k < tenants:
            pick = jnp.clip(bounds_ref[k, 1] - 1 - base, 0, toks - 1)
            first = bounds_ref[k, 0] - base
        else:
            pick = toks - 1
            first = start_at(base + toks - 1, bounds_ref) - base
        at = jnp.sum(jnp.where(lane == pick, logs, 0.0), axis=1, keepdims=True)
        inside = (lane <= pick) & (lane >= first)
        toward = jnp.exp(jnp.minimum(at - logs, 0.0) + jnp.where(inside, 0.0, NEG))
        carried = jnp.exp(at) * jnp.where(first < 0, 1.0, 0.0)
        lhs = jnp.concatenate(
            [
                (xdt_ref[h * hd : (h + 1) * hd, :] * toward[h : h + 1, :]).astype(BF16)
                for h in range(heads)
            ],
            axis=0,
        )
        state = jnp.dot(lhs, wide_b, preferred_element_type=F32)
        factor = jnp.concatenate(
            [jnp.broadcast_to(carried[h : h + 1, :], (hd, 128)) for h in range(heads)], axis=0
        )
        if k < tenants:
            local_ref[k * inner : (k + 1) * inner, :] = jnp.where(tok < 64, state, factor)
        else:
            high = factor.astype(BF16).astype(F32)
            packed = jnp.where(tok < 64, state, jnp.where(tok < 96, high, factor - high))
            pay_ref[:inner, :] = packed.astype(BF16)
    rows = [live[:, i * 128 : (i + 1) * 128] for i in range(toks // 128)]
    rows.append(jnp.zeros((16 - toks // 128, 128), F32))
    pay_ref[inner:, :] = jnp.concatenate(rows, axis=0).astype(BF16)


def gate_kernel(
    tenants,
    heads,
    bounds_ref,
    pay_ref,
    y_ref,
    z_refs,
    c_ref,
    entry_ref,
    local_ref,
    g_ref,
    tenant_ref,
):
    inner = y_ref.shape[0]
    half = z_refs[0].shape[1]
    hd = inner // heads
    incoming = jnp.zeros((inner, 64), F32)
    for block in range(pay_ref.shape[0] - 1):
        wide = pay_ref[block, :inner, :].astype(F32)
        passed = (wide[:, 64:65] + wide[:, 96:97]) * incoming + wide[:, :64]
        incoming = jnp.where(block < lax.axis_index("seq"), passed, incoming)
    for h in range(heads):
        rows = slice(h * hd, (h + 1) * hd)
        carry = jnp.dot(incoming[rows, :].astype(BF16), c_ref[...], preferred_element_type=F32)
        y_full = y_ref[rows, :] + carry * entry_ref[h : h + 1, :]
        for i, z_ref in enumerate(z_refs):
            here = slice(i * half, (i + 1) * half)
            g_ref[rows, here] = (y_full[:, here] * silu(z_ref[rows, :])).astype(BF16)
    for k in range(tenants):
        rows = slice(k * inner, (k + 1) * inner)
        last = bounds_ref[k, 1] - 1 - lax.axis_index("seq") * y_ref.shape[1]
        owned = jnp.where((last >= 0) & (last < y_ref.shape[1]), 1.0, 0.0)
        local = local_ref[rows, :]
        tenant_ref[rows, :] = ((local[:, 64:65] * incoming + local[:, :64]) * owned).astype(BF16)


def mixed_kernel(pieces, rows, *refs):
    slots_ref = refs[0]
    piece_refs = refs[1 : 1 + pieces]
    w_ref, hidden_refs, *out_refs, full_ref = refs[1 + pieces :]
    squares = lay_out(slots_ref, piece_refs, rows, full_ref)
    scale = lax.rsqrt(squares / full_ref.shape[0] + EPS)
    product = jnp.dot(w_ref[...], full_ref[...], preferred_element_type=F32) * scale
    half = out_refs[0].shape[1]
    for i, (hidden_ref, out_ref) in enumerate(zip(hidden_refs, out_refs, strict=True)):
        here = slice(i * half, (i + 1) * half)
        out_ref[...] = (hidden_ref[...].astype(F32) + product[:, here]).astype(BF16)


def qkv_kernel(rows, slots_ref, piece_refs, w_ref, first_refs, q_ref, kv_ref, all_refs, full_ref):
    squares = lay_out(slots_ref, piece_refs, rows, full_ref)
    scale = lax.rsqrt(squares / full_ref.shape[0] + EPS)
    product = jnp.dot(w_ref[...], full_ref[...], preferred_element_type=F32)
    att, half = q_ref.shape
    q_ref[...] = (product[:att] * scale).astype(BF16)
    kv_ref[...] = (product[att:] * scale).astype(BF16)
    for first_ref, all_ref in zip(first_refs, all_refs, strict=True):
        all_ref[:, :half] = first_ref[...]
        all_ref[:, half:] = kv_ref[...]


def attend_kernel(blocks, block_of, score_scale, *refs):
    bounds_ref, q_refs, kv_refs, pay_ref, seg_ref = refs[:5]
    ctx_ref, q_aug, k_aug, v_all, peak_ref, total_ref, sum_ref = refs[5:]
    inner = pay_ref.shape[1] - 16
    seq = lax.axis_index("seq")
    att, toks = ctx_ref.shape
    half = q_refs[0].shape[1]
    extra = q_aug.shape[0] - att
    row = lax.broadcasted_iota(jnp.int32, (extra, toks), 0)
    for i, q_ref in enumerate(q_refs):
        q_aug[:att, i * half : (i + 1) * half] = q_ref[...]
    q_aug[att:, :] = jnp.where(row == 0, 1.0, 0.0).astype(BF16)
    place = seq * toks + lax.broadcasted_iota(jnp.int32, (1, toks), 1)
    start = run_starts(seg_ref, bounds_ref)
    first_start = start_at(seq * toks, bounds_ref)
    peak_ref[...] = jnp.full(peak_ref.shape, NEG, F32)
    total_ref[...] = jnp.zeros(total_ref.shape, F32)
    sum_ref[...] = jnp.zeros(sum_ref.shape, F32)
    for b in range(blocks):
        block = block_of(b, seq)

        @pl.when((block >= 0) & (block <= seq) & (block * toks + toks > first_start))
        def _(b=b, block=block):
            count = toks
            for i, kv_ref in enumerate(kv_refs[b]):
                k_aug[:att, i * half : (i + 1) * half] = kv_ref[:att, :]
                v_all[:, i * half : (i + 1) * half] = kv_ref[att:, :]
            pads = pay_ref[block, inner:, :].astype(F32)
            pads = jnp.concatenate([pads[i : i + 1, :] for i in range(count // 128)], axis=1)
            bias = (pads - 1.0) * 1e30
            k_aug[att:, :] = jnp.where(row == 0, bias, 0.0).astype(BF16)
            scores = (
                lax.dot_general(
                    k_aug[...], q_aug[...], (((0,), (0,)), ((), ())), preferred_element_type=F32
                )
                * score_scale
            )
            key = block * count + lax.broadcasted_iota(jnp.int32, (count, toks), 0)
            scores = jnp.where((key <= place) & (key >= start), scores, NEG)
            peak = jnp.maximum(peak_ref[...], jnp.max(scores, axis=0, keepdims=True))
            weights = jnp.exp(scores - peak)
            keep = jnp.exp(peak_ref[...] - peak)
            peak_ref[...] = peak
            total_ref[...] = total_ref[...] * keep + jnp.sum(weights, axis=0, keepdims=True)
            sum_ref[...] = sum_ref[...] * keep + jnp.dot(
                v_all[...], weights.astype(BF16), preferred_element_type=F32
            )

    ctx_ref[...] = (sum_ref[...] / total_ref[...]).astype(BF16)


def last_kernel(pieces, rows, *refs):
    slots_ref = refs[0]
    piece_refs = refs[1 : 1 + pieces]
    w_ref, mixed_refs, out_ref, full_ref = refs[1 + pieces :]
    lay_out(slots_ref, piece_refs, rows, full_ref)
    product = jnp.dot(w_ref[...], full_ref[...], preferred_element_type=F32)
    half = mixed_refs[0].shape[1]
    for i, mixed_ref in enumerate(mixed_refs):
        here = slice(i * half, (i + 1) * half)
        out_ref[here, :] = (mixed_ref[...].astype(F32) + product[:, here]).T.astype(BF16)


def on_device(
    tp_count,
    seq_count,
    hidden_in,
    mamba_gain,
    w_xz,
    w_bc,
    w_dt,
    dt_bias,
    decay_rate,
    conv_x,
    conv_bc,
    skip_gain,
    inner_gain,
    w_out,
    attn_gain,
    w_qkv,
    w_o,
    seg_ids,
    pad_mask,
    tenant_bounds,
):
    toks, part = hidden_in.shape
    width = mamba_gain.shape[0]
    inner = w_xz.shape[1]
    heads = decay_rate.shape[0]
    att = w_qkv.shape[1]
    tenants = tenant_bounds.shape[0]
    bc = w_bc.shape[1]
    conv_rows = inner + bc
    seq = lax.axis_index("seq")
    sds = jax.ShapeDtypeStruct

    halves = 2
    half = toks // halves
    hidden_t = [hidden_in[i * half : (i + 1) * half].T for i in range(halves)]
    slots = jnp.asarray(sources(tp_count))
    seg_row, pad_row = seg_ids[None, :], pad_mask[None, :]

    out_share, o_share = inner // seq_count, att // seq_count

    def shares(first):
        out_rows, o_rows, _ = after((w_out, w_o), first)
        if out_share % 8 or o_share % 8:
            scaled = (out_rows.astype(F32) * inner_gain[:, None]).astype(BF16)
            cut = [
                lax.dynamic_slice_in_dim(rows, seq * count, count)
                for rows, count in ((scaled, out_share), (o_rows, o_share))
            ]
            return tuple(c.reshape(c.shape[0], tp_count, part).transpose(1, 0, 2) for c in cut)
        return pl.pallas_call(
            share_kernel,
            out_shape=(
                sds((tp_count, out_share, part), BF16),
                sds((tp_count, o_share, part), BF16),
            ),
            grid_spec=pltpu.PrefetchScalarGridSpec(
                num_scalar_prefetch=1,
                grid=(1,),
                in_specs=[
                    pl.BlockSpec((out_share, width), lambda i, at: (at[0], 0)),
                    pl.BlockSpec((o_share, width), lambda i, at: (at[0], 0)),
                    pl.BlockSpec((out_share, 128), lambda i, at: (at[0], 0)),
                ],
                out_specs=(
                    pl.BlockSpec((tp_count, out_share, part), lambda i, at: (0, 0, 0)),
                    pl.BlockSpec((tp_count, o_share, part), lambda i, at: (0, 0, 0)),
                ),
            ),
            compiler_params=pltpu.CompilerParams(vmem_limit_bytes=16 << 20),
        )(
            jnp.full((1,), seq, jnp.int32),
            out_rows,
            o_rows,
            jnp.broadcast_to(inner_gain[:, None], (inner, 128)),
        )

    in_rows = conv_rows + inner + 16

    def in_weights(first):
        xz, narrow, dt, _ = after((w_xz, w_bc, w_dt), first)
        return call(
            weights_kernel,
            sds((in_rows, width), BF16),
            (xz, narrow, dt, mamba_gain[None, :]),
            vmem=16,
            flops=10**7,
        )

    def exchange(share, first):
        value, _ = after((share,), first)
        return lax.all_to_all(value, "tp", 0, 0, tiled=False)

    def spread(columns, first):
        value, _ = after((columns,), first)
        return lax.all_gather(value, "seq", axis=1, tiled=True)

    full_in, ((out_shares, o_shares), w_in) = ring_gather(
        hidden_t, "tp", tp_count, ((1, 3, shares), (3, 5, in_weights))
    )
    pieces = len(full_in[0])

    raws, zs, dts, tails = zip(
        *(
            call(
                functools.partial(in_kernel, pieces, part, conv_rows, inner),
                (
                    sds((conv_rows, half), F32),
                    sds((inner, half), F32),
                    sds((8, half), F32),
                    sds((8, conv_rows), F32),
                ),
                (slots, *full, w_in),
                smem=(0,),
                scratch=[pltpu.VMEM((width, half), BF16), pltpu.VMEM((in_rows, half), F32)],
                flops=2 * in_rows * width * half,
            )
            for full in full_in
        ),
        strict=True,
    )
    tail = tails[-1]
    out_columns = exchange(out_shares, raws)
    halo = lax.ppermute(tail, "seq", [(i, i + 1) for i in range(seq_count - 1)])
    y, c_rows, entry, pay, local = call(
        functools.partial(mix_kernel, tenants, heads),
        (
            sds((inner, toks), F32),
            sds((bc // 2, toks), BF16),
            sds((8, toks), F32),
            sds((inner + 16, 128), BF16),
            sds((tenants * inner, 128), F32),
        ),
        (tenant_bounds, dt_bias, decay_rate, skip_gain, raws, dts, halo, conv_x, conv_bc, seg_row, pad_row),
        smem=(0, 1, 2, 3),
        scratch=[
            pltpu.VMEM((conv_rows, toks + 128), F32),
            pltpu.VMEM((conv_rows, toks), F32),
            pltpu.VMEM((inner, toks), F32),
            pltpu.VMEM((conv_rows, 128), F32),
        ],
        flops=10**9,
    )
    w_out_cols = spread(out_columns, pay)
    all_pays = lax.all_gather(pay, "seq", axis=0, tiled=False)
    gated, tenant_part = call(
        functools.partial(gate_kernel, tenants, heads),
        (
            sds((inner, toks), BF16),
            sds((tenants * inner, bc // 2), BF16),
        ),
        (tenant_bounds, all_pays, y, zs, c_rows, entry, local),
        smem=(0,),
        flops=10**8,
    )
    def tenant_sums(first):
        value, _ = after((tenant_part,), first)
        return sum_pairs(value, "seq", seq_count)

    def turned(cols, rows):
        def task(first):
            value, _ = after((cols,), first)
            return call(
                turn_kernel,
                sds((part, tp_count * rows), BF16),
                (value.reshape(tp_count * rows, part),),
            )

        return task

    (full_gated,), (tenant_sum, w_out_t) = ring_gather(
        [gated], "tp", tp_count, ((0, 2, tenant_sums), (3, -1, turned(w_out_cols, inner)))
    )
    tenant_states = tenant_sum.astype(F32).reshape(tenants, heads, inner // heads, bc // 2)
    mixed = call(
        functools.partial(mixed_kernel, len(full_gated), inner),
        [sds((part, half), BF16) for _ in range(halves)],
        (slots, *full_gated, w_out_t, hidden_t),
        smem=(0,),
        scratch=[pltpu.VMEM((tp_count * inner, toks), BF16)],
        flops=2 * part * tp_count * inner * toks,
    )

    def att_weights(first):
        value, _ = after((w_qkv,), first)
        return (value.reshape(3 * att, width).astype(F32) * attn_gain).astype(BF16)

    full_mixed, (w_att,) = ring_gather(mixed, "tp", tp_count, ((4, 5, att_weights),))
    queries, kvs = [], []
    for i, full in enumerate(full_mixed):
        last = i == halves - 1
        q_half, kv_half, whole = call(
            functools.partial(qkv_kernel, part),
            (
                sds((att, half), BF16),
                sds((2 * att, half), BF16),
                [sds((2 * att, toks), BF16)] if last else [],
            ),
            (slots, full, w_att, kvs if last else []),
            smem=(0,),
            scratch=[pltpu.VMEM((width, half), BF16)],
            flops=6 * att * width * half,
        )
        queries.append(q_half)
        kvs.append(kv_half)
    kv_cache = whole[0].reshape(2, att, toks)

    if seq_count == 4:

        def near(value):
            return lax.ppermute(value, "seq", [(0, 1), (2, 3)])

        def far(value):
            return lax.ppermute(value, "seq", [(0, 2), (1, 3)])

        def swap(value):
            return lax.ppermute(value, "seq", [(2, 3), (3, 2)])

        fars = [far(kv) for kv in kvs]
        nears = [near(kv) for kv in kvs]
        o_columns = exchange(o_shares, (fars, nears))
        swaps = [swap(kv) for kv in fars]
        w_o_cols = spread(o_columns, swaps)
        kv_blocks = [kvs, nears, fars, swaps]

        def block_of(b, at):
            return (at, at ^ 1, at - 2, (at ^ 1) - 2)[b]

    else:
        all_kv = [lax.all_gather(kv, "seq", axis=0, tiled=False) for kv in kvs]
        w_o_cols = spread(exchange(o_shares, kvs), kvs)
        kv_blocks = [[kv[i] for kv in all_kv] for i in range(seq_count)]

        def block_of(b, at):
            return jnp.int32(b)

    blocks = len(kv_blocks)
    deep = att + 32
    context = call(
        functools.partial(attend_kernel, blocks, block_of, att ** (-0.5)),
        sds((att, toks), BF16),
        (tenant_bounds, queries, kv_blocks, all_pays, seg_row),
        smem=(0,),
        scratch=[
            pltpu.VMEM((deep, toks), BF16),
            pltpu.VMEM((deep, toks), BF16),
            pltpu.VMEM((att, toks), BF16),
            pltpu.VMEM((1, toks), F32),
            pltpu.VMEM((1, toks), F32),
            pltpu.VMEM((att, toks), F32),
        ],
        flops=4 * blocks * toks * toks * att,
    )
    (full_context,), (w_o_t,) = ring_gather(
        [context], "tp", tp_count, ((1, 2, turned(w_o_cols, att)),)
    )
    hidden_out = call(
        functools.partial(last_kernel, len(full_context), att),
        sds((toks, part), BF16),
        (slots, *full_context, w_o_t, mixed),
        smem=(0,),
        scratch=[
            pltpu.VMEM((tp_count * att, toks), BF16),
        ],
        flops=2 * part * tp_count * att * toks,
    )
    return (hidden_out, kv_cache, tenant_states)


def solution(mesh):
    return jax.shard_map(
        functools.partial(on_device, mesh.shape["tp"], mesh.shape["seq"]),
        mesh=mesh,
        in_specs=(
            P("seq", "tp"),
            P(),
            P(None, "tp", None),
            P(),
            P("tp", None),
            P("tp"),
            P("tp"),
            P(None, "tp"),
            P(),
            P("tp"),
            P("tp"),
            P("tp", None),
            P(),
            P(None, "tp", None),
            P("tp", None),
            P("seq"),
            P("seq"),
            P(),
        ),
        out_specs=(P("seq", "tp"), P(None, "tp", "seq"), P(None, "tp", None, None)),
        check_vma=False,
    )
```
